512 devices in a mesh: shard: 32 (over z, core), tensor: 4 (over x), section: 4 (over y).
Axes of the slice: x: 4, y: 4, z: 16, core: 2. Of those that a mesh axis runs over, the one named last changes fastest.
Arguments:
- proj_grads: bfloat16 [4, 32, 2, 2048, 1024], P('section', 'shard', None, None, 'tensor'), as said below
- beta_grads: bfloat16 [4, 32, 2, 16, 2048], P('section', 'shard', None, 'tensor'), as said below
- gain_grads: bfloat16 [4, 32, 4, 2, 2048], P('section', 'shard', 'tensor'), as said below
- proj_master: float32 [4, 2048, 1024], P('section', 'shard', 'tensor'), may hold values from -0.25 to 0.25
- proj_moment: float32 [4, 2048, 1024], P('section', 'shard', 'tensor'), may hold values from -0.6 to 0.6
- proj_second: float32 [4, 2048, 1024], P('section', 'shard', 'tensor'), may hold values from 0.01 to 1
- beta_master: float32 [4, 16, 2048], P('section', 'tensor', 'shard'), may hold values from -0.25 to 0.25
- beta_moment: float32 [4, 16, 2048], P('section', 'tensor', 'shard'), may hold values from -0.6 to 0.6
- beta_second: float32 [4, 16, 2048], P('section', 'tensor', 'shard'), may hold values from 0.01 to 1
- gain_master: float32 [4, 2048], P('section', ('shard', 'tensor')), may hold values from 0.4 to 0.75
- gain_moment: float32 [4, 2048], P('section', ('shard', 'tensor')), may hold values from -0.6 to 0.6
- gain_second: float32 [4, 2048], P('section', ('shard', 'tensor')), may hold values from 0.01 to 1
- learn_rate: float32 [], replicated, may hold values from 0.01 to 0.04
- clip_limit: float32 [], replicated, may hold values from 730.063 to 2336.2016
Outputs:
- proj_weights: bfloat16 [4, 2048, 1024], P('section', None, 'tensor')
- beta_weights: bfloat16 [4, 16, 2048], P('section', 'tensor')
- gain_weights: bfloat16 [4, 2048], P('section')
- proj_master_new: float32 [4, 2048, 1024], P('section', 'shard', 'tensor')
- proj_moment_new: float32 [4, 2048, 1024], P('section', 'shard', 'tensor')
- proj_second_new: float32 [4, 2048, 1024], P('section', 'shard', 'tensor')
- beta_master_new: float32 [4, 16, 2048], P('section', 'tensor', 'shard')
- beta_moment_new: float32 [4, 16, 2048], P('section', 'tensor', 'shard')
- beta_second_new: float32 [4, 16, 2048], P('section', 'tensor', 'shard')
- gain_master_new: float32 [4, 2048], P('section', ('shard', 'tensor'))
- gain_moment_new: float32 [4, 2048], P('section', ('shard', 'tensor'))
- gain_second_new: float32 [4, 2048], P('section', ('shard', 'tensor'))
- grad_rms: float32 [], replicated
The draws below stay inside these ranges and needn't reach their ends.
Inputs may be any that keep to these rules, and one draw needn't show every extreme that they name: `proj_grads`: finite gradient values. `beta_grads`: finite gradient values. `gain_grads`: finite gradient values.
All inputs are finite; a program needn't handle non-finite values.
Results may differ from the reference program's by a relative error of at most 0.0005.
Values may be sent and summed in bfloat16 or wider, within the bound.
No kernel may reach another device: no remote copies, remote signals or barrier semaphores. Data moves between devices by JAX's collectives and lax.ppermute only.
A program may use at most 64 MiB of HBM per device.

```python
import math
import jax
import jax.numpy as jnp
from jax import lax

D = 2048
HEADS = 16
MB = 2
SECTIONS = 4
SHARDS = 32
TPAR = 4
PROJ_COLS = 1024
NUMEL = 8527872


def grad_block(key, sections, groups, micro, rows, cols, group_scale):
    keys = jax.random.split(key, 5)
    rise = 3.0
    if rows > 1:
        row_spread = 10.0 ** jax.random.uniform(keys[0], (rows,))
    else:
        row_spread = jnp.full((rows,), 4.64, jnp.float32)
    row_scale = row_spread * rise ** (jnp.arange(rows, dtype=jnp.float32) / rows)
    col_scale = 10.0 ** jax.random.uniform(keys[1], (cols,)) * rise ** (jnp.arange(cols, dtype=jnp.float32) / cols)
    section_scale = 9.0 ** jax.random.uniform(keys[4], (sections,))
    count = groups * micro

    def one_block(block_index):
        noise_key = jax.random.fold_in(keys[2], block_index)
        section_index = block_index // groups
        scale = 0.03 * group_scale * section_scale[section_index] * row_scale[:, None] * col_scale[None, :]
        values = jax.random.normal(noise_key, (micro, rows, cols)) / math.sqrt(count)
        return (values * scale).astype(jnp.bfloat16)
    blocks = lax.map(one_block, jnp.arange(sections * groups))
    return blocks.reshape(sections, groups, micro, rows, cols)


def draw_proj_grads(key, part):
    return grad_block(jax.random.fold_in(key, 101), SECTIONS, SHARDS, MB, D, PROJ_COLS, 1.0)


def draw_beta_grads(key, part):
    return grad_block(jax.random.fold_in(key, 202), SECTIONS, SHARDS, MB, HEADS, D, math.sqrt(PROJ_COLS / HEADS))


def draw_gain_grads(key, part):
    blocks = grad_block(jax.random.fold_in(key, 303), SECTIONS, SHARDS * TPAR, MB, 1, D, math.sqrt(PROJ_COLS))
    return blocks.reshape(SECTIONS, SHARDS, TPAR, MB, D)


def draw_clip_limit(key, part):
    unit = jax.random.uniform(jax.random.fold_in(key, 404), (), minval=0.0, maxval=1.0)
    low_end = 0.25
    high_end = 0.6
    scaled = jnp.exp(math.log(low_end) + unit * math.log(high_end / low_end))
    return (scaled * math.sqrt(NUMEL)).astype(jnp.float32)


def shard_levels(key, extent, cuts, low, top_value):
    gain, own = 1.0, jax.random.fold_in(key, 6)
    for dim, parts in cuts:
        draws = jnp.exp(jax.random.uniform(jax.random.fold_in(own, dim), (parts,), jnp.float32, low / len(cuts), top_value / len(cuts)))
        gain = gain * jnp.repeat(draws, extent[dim] // parts).reshape([-1 if axis == dim else 1 for axis in range(len(extent))])
    return gain


def scatter_about(own_key, dims, width, reach, pieces=(), kind=jnp.bfloat16):
    array = width * jax.random.normal(own_key, dims, jnp.float32)
    if pieces:
        array = array * shard_levels(own_key, dims, pieces, -0.22, 0.18)
    return jnp.clip(array, -reach, reach).astype(kind)


def setup_inputs(seed: int = 0) -> dict:
    arg_keys = jax.random.split(jax.random.key(seed), 15)
    proj_grads = draw_proj_grads(jax.random.fold_in(arg_keys[14], 71), 0)
    beta_grads = draw_beta_grads(jax.random.fold_in(arg_keys[14], 71), 0)
    gain_grads = draw_gain_grads(jax.random.fold_in(arg_keys[14], 71), 0)
    proj_master = scatter_about(arg_keys[3], (SECTIONS, D, PROJ_COLS), 0.05, 0.25, ((0, 4), (1, 32), (2, 4)), jnp.float32)
    proj_moment = scatter_about(arg_keys[4], (SECTIONS, D, PROJ_COLS), 0.1, 0.6, ((0, 4), (1, 32), (2, 4)), jnp.float32)
    proj_second = jnp.clip(jnp.exp(math.log(1.0) - 4.6051702 * jax.random.uniform(arg_keys[5], (SECTIONS, D, PROJ_COLS), jnp.float32) ** shard_levels(arg_keys[5], (SECTIONS, D, PROJ_COLS), ((0, 4), (1, 32), (2, 4)), -0.2, 0.2)), 0.01, 1.0)
    beta_master = scatter_about(arg_keys[6], (SECTIONS, HEADS, D), 0.05, 0.25, ((0, 4), (1, 4), (2, 32)), jnp.float32)
    beta_moment = scatter_about(arg_keys[7], (SECTIONS, HEADS, D), 0.1, 0.6, ((0, 4), (1, 4), (2, 32)), jnp.float32)
    beta_second = jnp.clip(jnp.exp(math.log(1.0) - 4.6051702 * jax.random.uniform(arg_keys[8], (SECTIONS, HEADS, D), jnp.float32) ** shard_levels(arg_keys[8], (SECTIONS, HEADS, D), ((0, 4), (1, 4), (2, 32)), -0.2, 0.2)), 0.01, 1.0)
    gain_master = jnp.clip(0.4 + 0.35 * jax.random.uniform(arg_keys[9], (SECTIONS, D), jnp.float32) ** shard_levels(arg_keys[9], (SECTIONS, D), ((0, 4), (1, 128)), -0.2, 0.2), 0.4, 0.75)
    gain_moment = scatter_about(arg_keys[10], (SECTIONS, D), 0.1, 0.6, ((0, 4), (1, 128)), jnp.float32)
    gain_second = jnp.clip(jnp.exp(math.log(1.0) - 4.6051702 * jax.random.uniform(arg_keys[11], (SECTIONS, D), jnp.float32) ** shard_levels(arg_keys[11], (SECTIONS, D), ((0, 4), (1, 128)), -0.2, 0.2)), 0.01, 1.0)
    learn_rate = jnp.clip(jnp.exp(jax.random.uniform(arg_keys[12], (), jnp.float32, math.log(0.01), math.log(0.04))), 0.01, 0.04)
    clip_limit = draw_clip_limit(jax.random.fold_in(arg_keys[14], 71), 0)
    return {"proj_grads": proj_grads, "beta_grads": beta_grads, "gain_grads": gain_grads, "proj_master": proj_master, "proj_moment": proj_moment, "proj_second": proj_second, "beta_master": beta_master, "beta_moment": beta_moment, "beta_second": beta_second, "gain_master": gain_master, "gain_moment": gain_moment, "gain_second": gain_second, "learn_rate": learn_rate, "clip_limit": clip_limit}


first_beta = 0.9
second_beta = 0.95
decay_rate = 0.1
adam_eps = 1e-08
norm_eps = 1e-06

def adam_update(grad, factor, learn_rate, master, moment, second):
    clipped = grad * factor
    moment_new = first_beta * moment + (1.0 - first_beta) * clipped
    second_new = second_beta * second + (1.0 - second_beta) * clipped * clipped
    master_new = master * (1.0 - learn_rate * decay_rate) - learn_rate * moment_new / (jnp.sqrt(second_new) + adam_eps)
    return (master_new, moment_new, second_new)

def reference(proj_grads, beta_grads, gain_grads, proj_master, proj_moment, proj_second, beta_master, beta_moment, beta_second, gain_master, gain_moment, gain_second, learn_rate, clip_limit):
    proj_total = lax.optimization_barrier(jnp.sum(proj_grads, axis=(1, 2), dtype=jnp.float32))
    beta_total = lax.optimization_barrier(jnp.sum(beta_grads, axis=(1, 2), dtype=jnp.float32))
    gain_total = lax.optimization_barrier(jnp.sum(gain_grads, axis=(1, 2, 3), dtype=jnp.float32))
    total_squares = jnp.sum(proj_total * proj_total) + jnp.sum(beta_total * beta_total) + jnp.sum(gain_total * gain_total)
    grad_rms = jnp.sqrt(total_squares / NUMEL)
    factor = jnp.minimum(1.0, clip_limit / (jnp.sqrt(total_squares) + norm_eps))
    proj_new = adam_update(proj_total, factor, learn_rate, proj_master, proj_moment, proj_second)
    beta_new = adam_update(beta_total, factor, learn_rate, beta_master, beta_moment, beta_second)
    gain_new = adam_update(gain_total, factor, learn_rate, gain_master, gain_moment, gain_second)
    return (proj_new[0].astype(jnp.bfloat16), beta_new[0].astype(jnp.bfloat16), gain_new[0].astype(jnp.bfloat16), proj_new[0], proj_new[1], proj_new[2], beta_new[0], beta_new[1], beta_new[2], gain_new[0], gain_new[1], gain_new[2], grad_rms)
```

```python
import jax
import jax.numpy as jnp
from jax import lax
from jax.sharding import Mesh
from jax.sharding import PartitionSpec as P

first_beta = 0.9
second_beta = 0.95
decay_rate = 0.1
adam_eps = 1e-08
norm_eps = 1e-06


def adam_update(grad, factor, learn_rate, master, moment, second):
    clipped = grad * factor
    moment_new = first_beta * moment + (1.0 - first_beta) * clipped
    second_new = second_beta * second + (1.0 - second_beta) * clipped * clipped
    master_new = master * (1.0 - learn_rate * decay_rate) - learn_rate * moment_new / (
        jnp.sqrt(second_new) + adam_eps
    )
    return (master_new, moment_new, second_new)


def per_device(
    proj_grads,
    beta_grads,
    gain_grads,
    proj_master,
    proj_moment,
    proj_second,
    beta_master,
    beta_moment,
    beta_second,
    gain_master,
    gain_moment,
    gain_second,
    learn_rate,
    clip_limit,
):
    chips = lax.axis_size("z")
    tensor_size = lax.axis_size("tensor")
    sections = lax.axis_size("section")
    core = lax.axis_index("core")
    tensor = lax.axis_index("tensor")
    section = lax.axis_index("section")
    width = proj_grads.shape[3]
    columns = proj_grads.shape[4]
    heads_here = beta_grads.shape[3]
    own = width // chips // 2
    lanes = 2 * own
    halves = columns // lanes

    proj_sum = jnp.sum(proj_grads[0, 0], axis=0, dtype=jnp.float32)
    beta_sum = jnp.sum(beta_grads[0, 0], axis=0, dtype=jnp.float32)
    gain_sum = jnp.sum(gain_grads[0, 0, 0], axis=0, dtype=jnp.float32)
    proj_blocks = proj_sum.reshape(chips, 2, own, halves, lanes).transpose(1, 0, 3, 2, 4)
    proj_blocks = proj_blocks.reshape(2, chips, halves * own, lanes)
    small = jnp.concatenate(
        [
            beta_sum.reshape(heads_here, chips, lanes).transpose(1, 0, 2),
            gain_sum.reshape(chips, 1, lanes),
            jnp.zeros((chips, 7 - heads_here, lanes), jnp.float32),
        ],
        axis=1,
    )
    packed = jnp.concatenate(
        [proj_blocks, jnp.broadcast_to(small[None], (2,) + small.shape)], axis=2
    )
    by_core = lax.all_to_all(packed, "core", 0, 0)
    by_chip = lax.all_to_all(by_core[0] + by_core[1], "z", 0, 0)
    total = jnp.sum(by_chip, axis=0)
    rows = halves * own
    proj_total = total[:rows].reshape(halves, own, lanes).transpose(1, 0, 2).reshape(own, columns)
    beta_wide = total[rows : rows + heads_here]
    gain_partial = total[rows + heads_here]

    lane = lax.iota(jnp.int32, lanes)
    mine = lane // own == core
    beta_total = lax.dynamic_slice_in_dim(beta_wide, core * own, own, axis=1)
    local_squares = jnp.sum(total[:rows] * total[:rows]) + jnp.sum(
        jnp.where(mine, beta_wide * beta_wide, 0.0)
    )

    share = gain_master.shape[1]
    slot = lane // share == core * tensor_size + tensor
    spread = lambda row: jnp.where(slot, jnp.tile(row[0], lanes // share), 0.0)
    message = jnp.stack(
        [
            gain_partial,
            jnp.full((lanes,), local_squares),
            spread(gain_master),
            spread(gain_moment),
            spread(gain_second),
            jnp.zeros((lanes,), jnp.float32),
            jnp.zeros((lanes,), jnp.float32),
            jnp.zeros((lanes,), jnp.float32),
        ]
    )
    peers = tensor_size * sections
    heard = lax.all_to_all(
        jnp.broadcast_to(message[None], (peers,) + message.shape), ("tensor", "section"), 0, 0
    )
    by_section = jnp.sum(heard.reshape((tensor_size, sections) + message.shape), axis=0)
    shard_squares = jnp.sum(by_section[:, 1, 0]) + jnp.sum(
        jnp.where(mine, by_section[:, 0] * by_section[:, 0], 0.0)
    )
    here = lax.broadcasted_iota(jnp.int32, (sections, 1, 1), 0) == section
    gain_rows = jnp.sum(jnp.where(here, by_section, 0.0), axis=0)

    shards = 2 * chips
    squares = lax.all_to_all(
        jnp.full((shards, 1, lanes), shard_squares), ("z", "core"), 0, 0
    )
    total_squares = jnp.sum(squares[:, 0, 0])
    counted = sections * (
        width * columns * tensor_size + heads_here * tensor_size * width + width
    )
    grad_rms = jnp.sqrt(total_squares / counted)
    factor = jnp.minimum(1.0, clip_limit / (jnp.sqrt(total_squares) + norm_eps))

    proj_new = adam_update(
        proj_total, factor, learn_rate, proj_master[0], proj_moment[0], proj_second[0]
    )
    beta_new = adam_update(
        beta_total, factor, learn_rate, beta_master[0], beta_moment[0], beta_second[0]
    )
    gain_new = adam_update(
        gain_rows[0], factor, learn_rate, gain_rows[2], gain_rows[3], gain_rows[4]
    )
    gain_own = [
        lax.dynamic_slice_in_dim(row, core * own + tensor * share, share)[None] for row in gain_new
    ]

    proj_half = proj_new[0].astype(jnp.bfloat16).reshape(own, halves, lanes).transpose(1, 0, 2)
    beta_half = jnp.where(mine, jnp.tile(beta_new[0].astype(jnp.bfloat16), (1, 2)), 0)
    gain_half = jnp.where(mine, gain_new[0].astype(jnp.bfloat16), 0)[None]
    weights = jnp.concatenate(
        [
            proj_half.reshape(rows, lanes),
            beta_half,
            gain_half,
            jnp.zeros((15 - heads_here, lanes), jnp.bfloat16),
        ],
        axis=0,
    )
    gathered = lax.all_gather(weights, "z", axis=0)
    other = lax.ppermute(gathered, "core", [(0, 1), (1, 0)])
    first = core == 0
    pair = jnp.stack([jnp.where(first, gathered, other), jnp.where(first, other, gathered)], axis=1)
    proj_weights = (
        pair[:, :, :rows]
        .reshape(chips, 2, halves, own, lanes)
        .transpose(0, 1, 3, 2, 4)
        .reshape(width, columns)
    )
    tail = jnp.where(mine, gathered[:, rows:], other[:, rows:])
    beta_weights = tail[:, :heads_here].transpose(1, 0, 2).reshape(heads_here, width)
    gain_weights = tail[:, heads_here].reshape(width)
    return (
        proj_weights[None],
        beta_weights[None],
        gain_weights[None],
        proj_new[0][None],
        proj_new[1][None],
        proj_new[2][None],
        beta_new[0][None],
        beta_new[1][None],
        beta_new[2][None],
        gain_own[0],
        gain_own[1],
        gain_own[2],
        grad_rms,
    )


def solution(mesh):
    shard, tensor, section = mesh.devices.shape
    split = Mesh(
        mesh.devices.reshape(shard // 2, 2, tensor, section), ("z", "core", "tensor", "section")
    )
    shard_axes = ("z", "core")
    all_axes = ("z", "core", "tensor")
    in_specs = (
        P("section", shard_axes, None, None, "tensor"),
        P("section", shard_axes, None, "tensor", None),
        P("section", shard_axes, "tensor", None, None),
        P("section", shard_axes, "tensor"),
        P("section", shard_axes, "tensor"),
        P("section", shard_axes, "tensor"),
        P("section", "tensor", shard_axes),
        P("section", "tensor", shard_axes),
        P("section", "tensor", shard_axes),
        P("section", all_axes),
        P("section", all_axes),
        P("section", all_axes),
        P(),
        P(),
    )
    out_specs = (
        P("section", None, "tensor"),
        P("section", "tensor", None),
        P("section", None),
        P("section", shard_axes, "tensor"),
        P("section", shard_axes, "tensor"),
        P("section", shard_axes, "tensor"),
        P("section", "tensor", shard_axes),
        P("section", "tensor", shard_axes),
        P("section", "tensor", shard_axes),
        P("section", all_axes),
        P("section", all_axes),
        P("section", all_axes),
        P(),
    )
    return jax.shard_map(
        per_device, mesh=split, in_specs=in_specs, out_specs=out_specs, check_vma=False
    )
```

```python
import jax
import jax.numpy as jnp
from jax import lax
from jax.experimental import pallas as pl
from jax.experimental.pallas import tpu as pltpu
from jax.sharding import PartitionSpec as P

first_beta = 0.9
second_beta = 0.95
decay_rate = 0.1
adam_eps = 1e-08
norm_eps = 1e-06

LANES = 128
TILE = 8
GROUP = 4

VMEM = pl.BlockSpec(memory_space=pltpu.VMEM)
SMEM = pl.BlockSpec(memory_space=pltpu.SMEM)


def adam_update(grad, factor, learn_rate, master, moment, second):
    clipped = grad * factor
    moment_new = first_beta * moment + (1.0 - first_beta) * clipped
    second_new = second_beta * second + (1.0 - second_beta) * clipped * clipped
    master_new = master * (1.0 - learn_rate * decay_rate) - learn_rate * moment_new / (
        jnp.sqrt(second_new) + adam_eps
    )
    return (master_new, moment_new, second_new)


def f32(shape):
    return jax.ShapeDtypeStruct(shape, jnp.float32)


def near_f32(shape):
    return pltpu.VMEM(shape, jnp.float32)


def held(value):
    return pltpu.with_memory_space_constraint(value, pltpu.VMEM)


def pack_kernel(core_ref, proj_ref, beta_ref, gain_ref, out_ref):
    heads_here = beta_ref.shape[1]
    own = proj_ref.shape[3]
    width = beta_ref.shape[2]
    residue = pl.program_id(0)
    tail = jnp.zeros((TILE - heads_here - 1, LANES), jnp.float32)
    for high in range(GROUP):
        rows = proj_ref[0, high, 0].astype(jnp.float32) + proj_ref[1, high, 0].astype(jnp.float32)
        for half in range(rows.shape[1] // LANES):
            out_ref[0, high, half * own : (half + 1) * own, :] = rows[
                :, half * LANES : (half + 1) * LANES
            ]
        start = pl.multiple_of((high * GROUP + residue) * LANES, LANES)
        columns = pl.ds(start, LANES)
        beta = beta_ref[0, :, columns].astype(jnp.float32) + beta_ref[1, :, columns].astype(
            jnp.float32
        )
        gain = gain_ref[:, columns].astype(jnp.float32)
        gain = gain[0:1] + gain[1:2]
        out_ref[0, high, 2 * own :, :] = jnp.concatenate([beta, gain, tail], axis=0)


def pack(which, proj, beta, gain, rows):
    own, columns = proj.shape[3:]
    return pl.pallas_call(
        pack_kernel,
        grid_spec=pltpu.PrefetchScalarGridSpec(
            num_scalar_prefetch=1,
            grid=(GROUP,),
            in_specs=[
                pl.BlockSpec(
                    (2, GROUP, 1, own, columns), lambda i, core: (0, 0, 2 * i + core[0], 0, 0)
                ),
                pl.BlockSpec(beta.shape, lambda i, core: (0, 0, 0)),
                pl.BlockSpec(gain.shape, lambda i, core: (0, 0)),
            ],
            out_specs=pl.BlockSpec((1, GROUP, rows, LANES), lambda i, core: (i, 0, 0, 0)),
        ),
        out_shape=f32((GROUP, GROUP, rows, LANES)),
        name="pack",
    )(which, proj, beta, gain)


def add_kernel(left_ref, right_ref, out_ref):
    out_ref[...] = left_ref[...] + right_ref[...]


def sum_kernel(in_ref, out_ref):
    out_ref[...] = (in_ref[0] + in_ref[1]) + (in_ref[2] + in_ref[3])


def norm_kernel(place_ref, in_ref, master_ref, moment_ref, second_ref, total_ref, message_ref):
    rows = total_ref.shape[0] - TILE
    own = LANES // 2
    heads_here = TILE // 2
    share = master_ref.shape[1]
    core, tensor = place_ref[0], place_ref[1]
    total = (in_ref[0] + in_ref[1]) + (in_ref[2] + in_ref[3])
    total_ref[...] = total
    proj = total[:rows]
    squares = proj * proj
    folded = squares[0:TILE]
    for row in range(TILE, rows, TILE):
        folded = folded + squares[row : row + TILE]
    tail = total[rows:]
    lane = lax.broadcasted_iota(jnp.int32, (TILE, LANES), 1)
    row = lax.broadcasted_iota(jnp.int32, (TILE, LANES), 0)
    mine = (lane // own == core) & (row < heads_here)
    folded = folded + jnp.where(mine, tail * tail, 0.0)
    local = jnp.sum(jnp.sum(folded, axis=0, keepdims=True), axis=1, keepdims=True)
    offset = core * own + tensor * share
    slot_from = lax.broadcasted_iota(jnp.int32, (share, LANES), 0)
    slot_to = lax.broadcasted_iota(jnp.int32, (share, LANES), 1)
    select = jnp.where(slot_from + offset == slot_to, 1.0, 0.0).astype(jnp.float32)
    spread = lambda ref: jnp.dot(
        ref[...], select, precision=lax.Precision.HIGHEST, preferred_element_type=jnp.float32
    )
    message = jnp.concatenate(
        [
            tail[heads_here : heads_here + 1],
            jnp.broadcast_to(local, (1, LANES)),
            spread(master_ref),
            spread(moment_ref),
            spread(second_ref),
            jnp.zeros((TILE - 5, LANES), jnp.float32),
        ],
        axis=0,
    )
    for peer in range(message_ref.shape[0]):
        message_ref[peer] = message


def section_kernel(place_ref, heard_ref, gain_ref, message_ref):
    core, section = place_ref[0], place_ref[2]
    own = LANES // 2
    sections = heard_ref.shape[0] // GROUP
    lane = lax.broadcasted_iota(jnp.int32, (TILE, LANES), 1)
    row = lax.broadcasted_iota(jnp.int32, (TILE, LANES), 0)
    mine = (lane // own == core) & (row == 0)
    counted = jnp.zeros((TILE, LANES), jnp.float32)
    here = jnp.zeros((TILE, LANES), jnp.float32)
    for other in range(sections):
        rows = heard_ref[other]
        for rank in range(1, GROUP):
            rows = rows + heard_ref[rank * sections + other]
        counted = counted + jnp.where(mine, rows * rows, 0.0)
        counted = counted + jnp.where((row == 1) & (lane == 0), rows, 0.0)
        here = here + jnp.where(section == other, rows, 0.0)
    gain_ref[...] = here
    total = jnp.sum(jnp.sum(counted, axis=0, keepdims=True), axis=1, keepdims=True)
    message_ref[...] = jnp.broadcast_to(total.reshape(1, 1, 1), message_ref.shape)


def update_kernel(
    place_ref,
    scalars_ref,
    squares_ref,
    total_ref,
    gain_ref,
    proj_master_ref,
    proj_moment_ref,
    proj_second_ref,
    beta_master_ref,
    beta_moment_ref,
    beta_second_ref,
    weights_ref,
    proj_master_out,
    proj_moment_out,
    proj_second_out,
    beta_master_out,
    beta_moment_out,
    beta_second_out,
    gain_master_out,
    gain_moment_out,
    gain_second_out,
    rms_ref,
    *,
    counted,
):
    core, tensor = place_ref[0], place_ref[1]
    own = proj_master_ref.shape[0]
    heads_here = beta_master_ref.shape[0]
    share = gain_master_out.shape[1]
    rows = total_ref.shape[0] - TILE
    rate = scalars_ref[0]
    squares = jnp.sum(squares_ref[...], axis=0)
    rms_ref[...] = jnp.sqrt(squares / counted)
    factor = jnp.minimum(1.0, scalars_ref[1] / (jnp.sqrt(squares) + norm_eps))
    for half in range(rows // own):
        columns = slice(half * LANES, (half + 1) * LANES)
        block = slice(half * own, (half + 1) * own)
        master, moment, second = adam_update(
            total_ref[block, :],
            factor,
            rate,
            proj_master_ref[:, columns],
            proj_moment_ref[:, columns],
            proj_second_ref[:, columns],
        )
        proj_master_out[:, columns] = master
        proj_moment_out[:, columns] = moment
        proj_second_out[:, columns] = second
        weights_ref[block, :] = master.astype(jnp.bfloat16)
    tail = pltpu.roll(total_ref[rows:, :], LANES - core * own, 1)
    beta = adam_update(
        tail[:heads_here, :own],
        factor[:, :own],
        rate,
        beta_master_ref[...],
        beta_moment_ref[...],
        beta_second_ref[...],
    )
    beta_master_out[...] = beta[0]
    beta_moment_out[...] = beta[1]
    beta_second_out[...] = beta[2]
    gain = adam_update(
        gain_ref[0:1], factor, rate, gain_ref[2:3], gain_ref[3:4], gain_ref[4:5]
    )
    stacked = jnp.concatenate(list(gain) + [jnp.zeros((TILE - 3, LANES), jnp.float32)], axis=0)
    rolled = pltpu.roll(stacked, LANES - core * own - tensor * share, 1)
    gain_master_out[...] = rolled[0:1, :share]
    gain_moment_out[...] = rolled[1:2, :share]
    gain_second_out[...] = rolled[2:3, :share]
    both = jnp.concatenate([beta[0], beta[0]], axis=1)
    weights_ref[rows:, :] = jnp.concatenate(
        [both, gain[0], jnp.zeros((2 * TILE - heads_here - 1, LANES), jnp.float32)], axis=0
    ).astype(jnp.bfloat16)


def spread_kernel(core_ref, mine_ref, other_ref, proj_ref, beta_ref, gain_ref):
    core = core_ref[0]
    chips = mine_ref.shape[0]
    own, columns = proj_ref.shape[2:]
    heads_here = beta_ref.shape[0]
    rows = own * (columns // LANES)
    lane = lax.broadcasted_iota(jnp.int32, (2 * TILE, LANES), 1)
    keep = lane // (LANES // 2) == core
    for chip in range(chips):
        for half in range(columns // LANES):
            block = slice(half * own, (half + 1) * own)
            lanes = slice(half * LANES, (half + 1) * LANES)
            proj_ref[chip, core, :, lanes] = mine_ref[chip, block, :]
            proj_ref[chip, 1 - core, :, lanes] = other_ref[chip, block, :]
        tail = jnp.where(
            keep,
            mine_ref[chip, rows:, :].astype(jnp.float32),
            other_ref[chip, rows:, :].astype(jnp.float32),
        ).astype(jnp.bfloat16)
        lanes = slice(chip * LANES, (chip + 1) * LANES)
        beta_ref[:, lanes] = tail[:heads_here]
        gain_ref[:, lanes] = tail[heads_here : heads_here + 1]


def per_device(
    proj_grads,
    beta_grads,
    gain_grads,
    proj_master,
    proj_moment,
    proj_second,
    beta_master,
    beta_moment,
    beta_second,
    gain_master,
    gain_moment,
    gain_second,
    learn_rate,
    clip_limit,
):
    shards = lax.axis_size("shard")
    tensor_size = lax.axis_size("tensor")
    sections = lax.axis_size("section")
    chips = shards // 2
    micro, width, columns = proj_grads.shape[2:]
    heads_here = beta_grads.shape[3]
    own = width // shards
    rows = own * (columns // LANES)
    core = lax.axis_index("shard") % 2
    place = jnp.stack([core, lax.axis_index("tensor"), lax.axis_index("section")]).astype(jnp.int32)

    core_pairs = [(s, s ^ 1) for s in range(shards)]
    near = []
    for side in range(2):
        for base in range(0, chips, GROUP):
            members = [(base + 2 * side + j) % chips for j in range(GROUP)]
            near.append([2 * z + side for z in sorted(members, key=lambda z: z % GROUP)])
    far = [
        [2 * (residue + high * GROUP) + side for high in range(chips // GROUP)]
        for side in range(2)
        for residue in range(GROUP)
    ]

    proj = proj_grads[0, 0].reshape(micro, chips // GROUP, 2 * GROUP, own, columns)
    beta = beta_grads[0, 0]
    gain = gain_grads[0, 0, 0]
    send = pack(1 - place[0:1], proj, beta, gain, rows + TILE)
    kept = pack(place[0:1], proj, beta, gain, rows + TILE)
    got = lax.ppermute(send, "shard", core_pairs)
    chip_sum = pl.pallas_call(
        add_kernel,
        out_shape=near_f32(kept.shape),
        in_specs=[VMEM, VMEM],
        out_specs=VMEM,
        name="core_add",
    )(kept, held(got))
    scalars = jnp.stack([learn_rate, clip_limit])
    chip_sum, place, scalars = lax.optimization_barrier((chip_sum, place, scalars))
    by_near = lax.all_to_all(chip_sum, "shard", 0, 0, axis_index_groups=near)
    near_sum = pl.pallas_call(
        sum_kernel, out_shape=near_f32(by_near.shape[1:]), in_specs=[VMEM], out_specs=VMEM, name="near"
    )(held(by_near))
    by_far = lax.all_to_all(near_sum, "shard", 0, 0, axis_index_groups=far)
    peers = tensor_size * sections
    total, message = pl.pallas_call(
        norm_kernel,
        out_shape=(near_f32((rows + TILE, LANES)), near_f32((peers, TILE, LANES))),
        in_specs=[SMEM] + [VMEM] * 4,
        out_specs=(VMEM, VMEM),
        name="norm",
    )(place, held(by_far), gain_master, gain_moment, gain_second)
    heard = lax.all_to_all(message, ("tensor", "section"), 0, 0)
    gain_rows, squares = pl.pallas_call(
        section_kernel,
        out_shape=(near_f32((TILE, LANES)), near_f32((shards, 1, LANES))),
        in_specs=[SMEM, VMEM],
        out_specs=(VMEM, VMEM),
        name="section",
    )(place, held(heard))
    squares = lax.all_to_all(squares, "shard", 0, 0)
    counted = sections * (
        width * columns * tensor_size + heads_here * tensor_size * width + width
    )
    state = f32((own, columns))
    beta_state = f32((heads_here, own))
    gain_state = f32(gain_master.shape)
    outs = pl.pallas_call(
        lambda *refs: update_kernel(*refs, counted=float(counted)),
        out_shape=(pltpu.VMEM((rows + 2 * TILE, LANES), jnp.bfloat16),)
        + (state,) * 3
        + (beta_state,) * 3
        + (gain_state,) * 3
        + (f32((1, LANES)),),
        in_specs=[SMEM] * 2 + [VMEM] * 9,
        out_specs=(VMEM,) * 11,
        name="update",
    )(
        place,
        scalars,
        held(squares),
        held(total),
        held(gain_rows),
        proj_master[0],
        proj_moment[0],
        proj_second[0],
        beta_master[0],
        beta_moment[0],
        beta_second[0],
    )
    z_groups = [[2 * z + side for z in range(chips)] for side in range(2)]
    gathered = lax.all_gather(outs[0], "shard", axis=0, axis_index_groups=z_groups)
    other = lax.ppermute(gathered, "shard", core_pairs)
    proj_weights, beta_weights, gain_weights = pl.pallas_call(
        spread_kernel,
        out_shape=(
            jax.ShapeDtypeStruct((chips, 2, own, columns), jnp.bfloat16),
            jax.ShapeDtypeStruct((heads_here, width), jnp.bfloat16),
            jax.ShapeDtypeStruct((1, width), jnp.bfloat16),
        ),
        in_specs=[SMEM, VMEM, VMEM],
        out_specs=(VMEM,) * 3,
        name="spread",
    )(place, held(gathered), held(other))
    return (
        proj_weights.reshape(1, width, columns),
        beta_weights[None],
        gain_weights,
        outs[1][None],
        outs[2][None],
        outs[3][None],
        outs[4][None],
        outs[5][None],
        outs[6][None],
        outs[7],
        outs[8],
        outs[9],
        outs[10][0, 0],
    )


def solution(mesh):
    in_specs = (
        P("section", "shard", None, None, "tensor"),
        P("section", "shard", None, "tensor", None),
        P("section", "shard", "tensor", None, None),
        P("section", "shard", "tensor"),
        P("section", "shard", "tensor"),
        P("section", "shard", "tensor"),
        P("section", "tensor", "shard"),
        P("section", "tensor", "shard"),
        P("section", "tensor", "shard"),
        P("section", ("shard", "tensor")),
        P("section", ("shard", "tensor")),
        P("section", ("shard", "tensor")),
        P(),
        P(),
    )
    out_specs = (
        P("section", None, "tensor"),
        P("section", "tensor", None),
        P("section", None),
        P("section", "shard", "tensor"),
        P("section", "shard", "tensor"),
        P("section", "shard", "tensor"),
        P("section", "tensor", "shard"),
        P("section", "tensor", "shard"),
        P("section", "tensor", "shard"),
        P("section", ("shard", "tensor")),
        P("section", ("shard", "tensor")),
        P("section", ("shard", "tensor")),
        P(),
    )
    return jax.shard_map(
        per_device, mesh=mesh, in_specs=in_specs, out_specs=out_specs, check_vma=False
    )
```

```python
import functools

import jax
import jax.numpy as jnp
from jax import lax
from jax.experimental import pallas as pl
from jax.experimental.pallas import tpu as pltpu
from jax.sharding import PartitionSpec as P

first_beta = 0.9
second_beta = 0.95
decay_rate = 0.1
adam_eps = 1e-08
norm_eps = 1e-06

LANES = 128
TILE = 8
GROUP = 4
WIRE = jnp.float16
WIRE_SCALE = 2.0**15

VMEM = pl.BlockSpec(memory_space=pltpu.VMEM)
SMEM = pl.BlockSpec(memory_space=pltpu.SMEM)


def adam_update(grad, factor, learn_rate, master, moment, second):
    clipped = grad * factor
    moment_new = first_beta * moment + (1.0 - first_beta) * clipped
    second_new = second_beta * second + (1.0 - second_beta) * clipped * clipped
    master_new = master * (1.0 - learn_rate * decay_rate) - learn_rate * moment_new / (
        jnp.sqrt(second_new) + adam_eps
    )
    return (master_new, moment_new, second_new)


def f32(shape):
    return jax.ShapeDtypeStruct(shape, jnp.float32)


def near_f32(shape):
    return pltpu.VMEM(shape, jnp.float32)


def held(value):
    return pltpu.with_memory_space_constraint(value, pltpu.VMEM)


def pack_kernel(rate_ref, clip_ref, proj_ref, beta_ref, gain_ref, out_ref, scalars_ref, buffer, arrived, *, flip):
    heads_here = beta_ref.shape[1]
    own = proj_ref.shape[3]
    core = lax.axis_index("shard") % 2
    which = 1 - core if flip else core
    copies = [
        pltpu.make_async_copy(
            proj_ref.at[:, :, 2 * residue + which], buffer.at[residue], arrived.at[residue]
        )
        for residue in range(GROUP)
    ]
    for copy in copies:
        copy.start()
    lane = lax.broadcasted_iota(jnp.int32, scalars_ref.shape, 0)
    scalars_ref[...] = jnp.where(lane == 0, rate_ref[0], clip_ref[0])
    beta = beta_ref[0].astype(jnp.float32) + beta_ref[1].astype(jnp.float32)
    gain = gain_ref[...].astype(jnp.float32)
    gain = gain[0:1] + gain[1:2]
    blank = jnp.zeros((TILE - heads_here - 1, LANES), jnp.float32)
    for chip in range(GROUP * GROUP):
        columns = slice(chip * LANES, (chip + 1) * LANES)
        out_ref[chip % GROUP, chip // GROUP, 2 * own :, :] = jnp.concatenate(
            [beta[:, columns], gain[:, columns], blank], axis=0
        )
    for residue in range(GROUP):
        copies[residue].wait()
        for high in range(GROUP):
            rows = buffer[residue, 0, high].astype(jnp.float32) + buffer[residue, 1, high].astype(
                jnp.float32
            )
            for half in range(rows.shape[1] // LANES):
                out_ref[residue, high, half * own : (half + 1) * own, :] = rows[
                    :, half * LANES : (half + 1) * LANES
                ]


def pack(flip, rate, clip, proj, beta, gain, rows):
    own, columns = proj.shape[3:]
    return pl.pallas_call(
        functools.partial(pack_kernel, flip=flip),
        in_specs=[SMEM, SMEM, pl.BlockSpec(memory_space=pl.ANY), VMEM, VMEM],
        out_specs=(VMEM, VMEM),
        out_shape=(f32((GROUP, GROUP, rows, LANES)), near_f32((TILE, LANES))),
        scratch_shapes=[
            pltpu.VMEM((GROUP, 2, GROUP, own, columns), jnp.bfloat16),
            pltpu.SemaphoreType.DMA((GROUP,)),
        ],
        name="pack",
    )(rate, clip, proj, beta, gain)


def add_kernel(left_ref, right_ref, out_ref):
    out_ref[...] = left_ref[...] + right_ref[...]


def sum_kernel(in_ref, out_ref):
    out_ref[...] = (in_ref[0] + in_ref[1]) + (in_ref[2] + in_ref[3])


def norm_kernel(in_ref, master_ref, moment_ref, second_ref, total_ref, message_ref):
    rows = total_ref.shape[0] - TILE
    own = LANES // 2
    heads_here = TILE // 2
    share = master_ref.shape[1]
    core = lax.axis_index("shard") % 2
    total = (in_ref[0] + in_ref[1]) + (in_ref[2] + in_ref[3])
    tail = pltpu.roll(total[rows:], LANES - core * own, 1)
    total_ref[:rows, :] = total[:rows]
    total_ref[rows:, :] = tail
    squares = total[:rows] * total[:rows]
    folded = squares[0:TILE]
    for row in range(TILE, rows, TILE):
        folded = folded + squares[row : row + TILE]
    lane = lax.broadcasted_iota(jnp.int32, (TILE, LANES), 1)
    row = lax.broadcasted_iota(jnp.int32, (TILE, LANES), 0)
    folded = folded + jnp.where((lane < own) & (row < heads_here), tail * tail, 0.0)
    local = jnp.sum(jnp.sum(folded, axis=0, keepdims=True), axis=1, keepdims=True)
    state = jnp.concatenate(
        [
            jnp.zeros((1, LANES - 3 * share), jnp.float32),
            master_ref[...],
            moment_ref[...],
            second_ref[...],
        ],
        axis=1,
    )
    lane = lane[0:1]
    message = jnp.where(
        lane < own,
        tail[heads_here : heads_here + 1],
        jnp.where(lane == own, local, state),
    )
    for peer in range(message_ref.shape[0]):
        message_ref[peer] = message


def section_kernel(heard_ref, gain_ref, message_ref):
    section = lax.axis_index("section")
    own = LANES // 2
    sections = heard_ref.shape[0] // GROUP
    share = own // GROUP
    lane = lax.broadcasted_iota(jnp.int32, (1, LANES), 1)
    counted = jnp.zeros((1, LANES), jnp.float32)
    here = jnp.zeros((1, LANES), jnp.float32)
    ranks = [jnp.zeros((1, LANES), jnp.float32) for _ in range(GROUP)]
    for other in range(sections):
        rows = [heard_ref[rank * sections + other] for rank in range(GROUP)]
        summed = (rows[0] + rows[1]) + (rows[2] + rows[3])
        counted = counted + jnp.where(
            lane < own, summed * summed, jnp.where(lane == own, summed, 0.0)
        )
        here = here + jnp.where(section == other, summed, 0.0)
        ranks = [
            rank + jnp.where(section == other, row, 0.0) for rank, row in zip(ranks, rows)
        ]
    gain_ref[0:1, :] = here
    for kind in range(3):
        start = LANES - (3 - kind) * share
        state = jnp.ones((1, LANES), jnp.float32)
        for rank in range(GROUP):
            moved = pltpu.roll(ranks[rank], (rank * share - start) % LANES, 1)
            state = jnp.where(lane // share == rank, moved, state)
        gain_ref[kind + 1 : kind + 2, :] = state
    gain_ref[4:, :] = jnp.zeros((TILE - 4, LANES), jnp.float32)
    total = jnp.broadcast_to(jnp.sum(counted, axis=1, keepdims=True), (1, LANES))
    for peer in range(message_ref.shape[0]):
        message_ref[peer] = total


def update_kernel(
    scalars_ref,
    squares_ref,
    total_ref,
    gain_ref,
    proj_master_ref,
    proj_moment_ref,
    proj_second_ref,
    beta_master_ref,
    beta_moment_ref,
    beta_second_ref,
    weights_ref,
    proj_master_out,
    proj_moment_out,
    proj_second_out,
    beta_master_out,
    beta_moment_out,
    beta_second_out,
    gain_master_out,
    gain_moment_out,
    gain_second_out,
    rms_ref,
    *,
    counted,
):
    core, tensor = lax.axis_index("shard") % 2, lax.axis_index("tensor")
    own = proj_master_ref.shape[0]
    heads_here = beta_master_ref.shape[0]
    share = gain_master_out.shape[1]
    rows = total_ref.shape[0] - TILE
    rate = scalars_ref[0:1, :]
    squares = jnp.sum(squares_ref[...], axis=0)
    rms_ref[...] = jnp.sqrt(squares / counted)
    factor = jnp.minimum(1.0, scalars_ref[1:2, :] / (jnp.sqrt(squares) + norm_eps))
    for half in range(rows // own):
        columns = slice(half * LANES, (half + 1) * LANES)
        block = slice(half * own, (half + 1) * own)
        master, moment, second = adam_update(
            total_ref[block, :],
            factor,
            rate,
            proj_master_ref[:, columns],
            proj_moment_ref[:, columns],
            proj_second_ref[:, columns],
        )
        proj_master_out[:, columns] = master
        proj_moment_out[:, columns] = moment
        proj_second_out[:, columns] = second
        weights_ref[:own, columns] = master.astype(jnp.bfloat16)
    beta = adam_update(
        total_ref[rows : rows + heads_here, :own],
        factor[:, :own],
        rate[:, :own],
        beta_master_ref[...],
        beta_moment_ref[...],
        beta_second_ref[...],
    )
    beta_master_out[...] = beta[0]
    beta_moment_out[...] = beta[1]
    beta_second_out[...] = beta[2]
    gain = adam_update(
        gain_ref[0:1], factor, rate, gain_ref[1:2], gain_ref[2:3], gain_ref[3:4]
    )
    stacked = jnp.concatenate(list(gain) + [jnp.zeros((TILE - 3, LANES), jnp.float32)], axis=0)
    rolled = pltpu.roll(stacked, LANES - tensor * share, 1)
    gain_master_out[...] = rolled[0:1, :share]
    gain_moment_out[...] = rolled[1:2, :share]
    gain_second_out[...] = rolled[2:3, :share]
    small = jnp.concatenate(
        [beta[0], gain[0][:, :own], jnp.zeros((TILE - heads_here - 1, own), jnp.float32)], axis=0
    )
    small = jnp.concatenate([small, small], axis=1).astype(jnp.bfloat16)
    weights_ref[own:, :LANES] = small
    weights_ref[own:, LANES:] = jnp.zeros_like(small)


def unpack_kernel(in_ref, beta_ref, gain_ref):
    heads_here = beta_ref.shape[0]
    first = lax.broadcasted_iota(jnp.int32, (TILE, LANES), 1) < LANES // 2
    for chip in range(in_ref.shape[0] // 2):
        small = jnp.where(
            first,
            in_ref[2 * chip].astype(jnp.float32),
            in_ref[2 * chip + 1].astype(jnp.float32),
        ).astype(jnp.bfloat16)
        columns = slice(chip * LANES, (chip + 1) * LANES)
        beta_ref[:, columns] = small[:heads_here]
        gain_ref[:, columns] = small[heads_here : heads_here + 1]


def per_device(
    proj_grads,
    beta_grads,
    gain_grads,
    proj_master,
    proj_moment,
    proj_second,
    beta_master,
    beta_moment,
    beta_second,
    gain_master,
    gain_moment,
    gain_second,
    learn_rate,
    clip_limit,
):
    shards = lax.axis_size("shard")
    tensor_size = lax.axis_size("tensor")
    sections = lax.axis_size("section")
    chips = shards // 2
    micro, width, columns = proj_grads.shape[2:]
    heads_here = beta_grads.shape[3]
    own = width // shards
    rows = own * (columns // LANES)
    core_pairs = [(s, s ^ 1) for s in range(shards)]
    near = []
    for side in range(2):
        for base in range(0, chips, GROUP):
            members = [(base + 2 * side + j) % chips for j in range(GROUP)]
            near.append([2 * z + side for z in sorted(members, key=lambda z: z % GROUP)])
    far = [
        [2 * (residue + high * GROUP) + side for high in range(chips // GROUP)]
        for side in range(2)
        for residue in range(GROUP)
    ]

    proj = proj_grads[0, 0].reshape(micro, chips // GROUP, 2 * GROUP, own, columns)
    beta = beta_grads[0, 0]
    gain = gain_grads[0, 0, 0]
    rate, clip = learn_rate.reshape(1), clip_limit.reshape(1)
    send, _ = pack(True, rate, clip, proj, beta, gain, rows + TILE)
    kept, scalars = pack(False, rate, clip, proj, beta, gain, rows + TILE)
    got = lax.ppermute(send, "shard", core_pairs)
    chip_sum = pl.pallas_call(
        add_kernel,
        out_shape=near_f32(kept.shape),
        in_specs=[VMEM, VMEM],
        out_specs=VMEM,
        name="core_add",
    )(kept, held(got))
    by_near = lax.all_to_all(chip_sum, "shard", 0, 0, axis_index_groups=near)
    near_sum = pl.pallas_call(
        sum_kernel, out_shape=near_f32(by_near.shape[1:]), in_specs=[VMEM], out_specs=VMEM, name="near"
    )(held(by_near))
    by_far = lax.all_to_all(near_sum, "shard", 0, 0, axis_index_groups=far)
    peers = tensor_size * sections
    total, message = pl.pallas_call(
        norm_kernel,
        out_shape=(near_f32((rows + TILE, LANES)), near_f32((peers, 1, LANES))),
        in_specs=[VMEM] * 4,
        out_specs=(VMEM, VMEM),
        name="norm",
    )(held(by_far), gain_master, gain_moment, gain_second)
    heard = lax.all_to_all(message, ("tensor", "section"), 0, 0)
    gain_rows, squares = pl.pallas_call(
        section_kernel,
        out_shape=(near_f32((TILE, LANES)), near_f32((shards, 1, LANES))),
        in_specs=[VMEM],
        out_specs=(VMEM, VMEM),
        name="section",
    )(held(heard))
    squares = lax.all_to_all(squares, "shard", 0, 0)
    counted = sections * (
        width * columns * tensor_size + heads_here * tensor_size * width + width
    )
    state = f32((own, columns))
    beta_state = f32((heads_here, own))
    gain_state = f32(gain_master.shape)
    outs = pl.pallas_call(
        functools.partial(update_kernel, counted=float(counted)),
        out_shape=(pltpu.VMEM((own + TILE, columns), jnp.bfloat16),)
        + (state,) * 3
        + (beta_state,) * 3
        + (gain_state,) * 3
        + (f32((1, LANES)),),
        in_specs=[VMEM] * 10,
        out_specs=(VMEM,) * 11,
        name="update",
    )(
        held(scalars),
        held(squares),
        held(total),
        held(gain_rows),
        proj_master[0],
        proj_moment[0],
        proj_second[0],
        beta_master[0],
        beta_moment[0],
        beta_second[0],
    )
    sent = (outs[0].astype(jnp.float32) * WIRE_SCALE).astype(WIRE)
    gathered = lax.all_gather(sent, "shard", axis=0)
    unscaled = lambda value: (value.astype(jnp.float32) * (1.0 / WIRE_SCALE)).astype(jnp.bfloat16)
    proj_weights = unscaled(gathered[:, :own])
    small = unscaled(gathered[:, own:, :LANES])
    beta_weights, gain_weights = pl.pallas_call(
        unpack_kernel,
        out_shape=(
            jax.ShapeDtypeStruct((heads_here, width), jnp.bfloat16),
            jax.ShapeDtypeStruct((1, width), jnp.bfloat16),
        ),
        in_specs=[VMEM],
        out_specs=(VMEM, VMEM),
        name="unpack",
    )(held(small))
    return (
        proj_weights.reshape(1, width, columns),
        beta_weights[None],
        gain_weights,
        outs[1][None],
        outs[2][None],
        outs[3][None],
        outs[4][None],
        outs[5][None],
        outs[6][None],
        outs[7],
        outs[8],
        outs[9],
        outs[10][0, 0],
    )


def solution(mesh):
    in_specs = (
        P("section", "shard", None, None, "tensor"),
        P("section", "shard", None, "tensor", None),
        P("section", "shard", "tensor", None, None),
        P("section", "shard", "tensor"),
        P("section", "shard", "tensor"),
        P("section", "shard", "tensor"),
        P("section", "tensor", "shard"),
        P("section", "tensor", "shard"),
        P("section", "tensor", "shard"),
        P("section", ("shard", "tensor")),
        P("section", ("shard", "tensor")),
        P("section", ("shard", "tensor")),
        P(),
        P(),
    )
    out_specs = (
        P("section", None, "tensor"),
        P("section", "tensor", None),
        P("section", None),
        P("section", "shard", "tensor"),
        P("section", "shard", "tensor"),
        P("section", "shard", "tensor"),
        P("section", "tensor", "shard"),
        P("section", "tensor", "shard"),
        P("section", "tensor", "shard"),
        P("section", ("shard", "tensor")),
        P("section", ("shard", "tensor")),
        P("section", ("shard", "tensor")),
        P(),
    )
    return jax.shard_map(
        per_device, mesh=mesh, in_specs=in_specs, out_specs=out_specs, check_vma=False
    )
```

```python
import functools

import jax
import jax.numpy as jnp
from jax import lax
from jax.experimental import pallas as pl
from jax.experimental.pallas import tpu as pltpu
from jax.sharding import PartitionSpec as P

first_beta = 0.9
second_beta = 0.95
decay_rate = 0.1
adam_eps = 1e-08
norm_eps = 1e-06

LANES = 128
TILE = 8
GROUP = 4
CODE_TOP = 14.0
CODE_STEP = 1.5 * 2.0**27
WIRE = jnp.float16
WIRE_SCALE = 2.0**15

VMEM = pl.BlockSpec(memory_space=pltpu.VMEM)
SMEM = pl.BlockSpec(memory_space=pltpu.SMEM)


def adam_update(grad, factor, learn_rate, master, moment, second):
    clipped = grad * factor
    moment_new = first_beta * moment + (1.0 - first_beta) * clipped
    second_new = second_beta * second + (1.0 - second_beta) * clipped * clipped
    master_new = master * (1.0 - learn_rate * decay_rate) - learn_rate * moment_new / (
        jnp.sqrt(second_new) + adam_eps
    )
    return (master_new, moment_new, second_new)


def f32(shape):
    return jax.ShapeDtypeStruct(shape, jnp.float32)


def near_f32(shape):
    return pltpu.VMEM(shape, jnp.float32)


def held(value):
    return pltpu.with_memory_space_constraint(value, pltpu.VMEM)


def pack_kernel(rate_ref, clip_ref, proj_ref, beta_ref, gain_ref, out_ref, scalars_ref, buffer, arrived, *, flip):
    heads_here = beta_ref.shape[1]
    own = proj_ref.shape[3]
    core = lax.axis_index("shard") % 2
    which = 1 - core if flip else core
    copies = [
        pltpu.make_async_copy(
            proj_ref.at[:, :, 2 * residue + which], buffer.at[residue], arrived.at[residue]
        )
        for residue in range(GROUP)
    ]
    for copy in copies:
        copy.start()
    lane = lax.broadcasted_iota(jnp.int32, scalars_ref.shape, 0)
    scalars_ref[...] = jnp.where(lane == 0, rate_ref[0], clip_ref[0])
    beta = beta_ref[0].astype(jnp.float32) + beta_ref[1].astype(jnp.float32)
    gain = gain_ref[...].astype(jnp.float32)
    gain = gain[0:1] + gain[1:2]
    blank = jnp.zeros((TILE - heads_here - 1, LANES), jnp.float32)
    for chip in range(GROUP * GROUP):
        columns = slice(chip * LANES, (chip + 1) * LANES)
        out_ref[chip % GROUP, chip // GROUP, 2 * own :, :] = jnp.concatenate(
            [beta[:, columns], gain[:, columns], blank], axis=0
        )
    for residue in range(GROUP):
        copies[residue].wait()
        for high in range(GROUP):
            rows = buffer[residue, 0, high].astype(jnp.float32) + buffer[residue, 1, high].astype(
                jnp.float32
            )
            for half in range(rows.shape[1] // LANES):
                out_ref[residue, high, half * own : (half + 1) * own, :] = rows[
                    :, half * LANES : (half + 1) * LANES
                ]


def pack(flip, rate, clip, proj, beta, gain, rows):
    own, columns = proj.shape[3:]
    return pl.pallas_call(
        functools.partial(pack_kernel, flip=flip),
        in_specs=[SMEM, SMEM, pl.BlockSpec(memory_space=pl.ANY), VMEM, VMEM],
        out_specs=(VMEM, VMEM),
        out_shape=(f32((GROUP, GROUP, rows, LANES)), near_f32((TILE, LANES))),
        scratch_shapes=[
            pltpu.VMEM((GROUP, 2, GROUP, own, columns), jnp.bfloat16),
            pltpu.SemaphoreType.DMA((GROUP,)),
        ],
        name="pack",
    )(rate, clip, proj, beta, gain)


def block_scale(rows):
    largest = jnp.max(jnp.max(jnp.abs(rows), axis=0, keepdims=True), axis=1, keepdims=True)
    return jnp.ceil(jnp.log2(jnp.maximum(largest, 1e-30)) + 0.01)


def code_kernel(left_ref, right_ref, out_ref):
    rows = left_ref.shape[2] - TILE
    row = lax.broadcasted_iota(jnp.int32, (TILE, LANES), 0)
    for chip in range(GROUP * GROUP):
        place = (chip % GROUP, chip // GROUP)
        proj = left_ref[place + (slice(0, rows),)] + right_ref[place + (slice(0, rows),)]
        tail = left_ref[place + (slice(rows, None),)] + right_ref[place + (slice(rows, None),)]
        proj_scale, tail_scale = block_scale(proj), block_scale(tail)
        out_ref[chip, :rows, :] = proj * jnp.exp2(CODE_TOP - proj_scale)
        tail = tail * jnp.exp2(CODE_TOP - tail_scale)
        high = (tail + CODE_STEP) - CODE_STEP
        low = tail - high
        high = jnp.where(row == TILE - 2, proj_scale, jnp.where(row == TILE - 1, tail_scale, high))
        out_ref[chip, rows : rows + TILE, :] = high
        out_ref[chip, rows + TILE :, :] = low


def add_kernel(left_ref, right_ref, out_ref):
    out_ref[...] = left_ref[...] + right_ref[...]


def sum_kernel(in_ref, out_ref):
    out_ref[...] = (in_ref[0] + in_ref[1]) + (in_ref[2] + in_ref[3])


def norm_message(total, failed, master_ref, moment_ref, second_ref, total_ref, message_ref):
    rows = total_ref.shape[0] - TILE
    own = LANES // 2
    heads_here = TILE // 2
    share = master_ref.shape[1]
    core = lax.axis_index("shard") % 2
    tail = pltpu.roll(total[rows:], LANES - core * own, 1)
    total_ref[:rows, :] = total[:rows]
    total_ref[rows:, :] = tail
    folded = fold(total[:rows] * total[:rows])
    lane = lax.broadcasted_iota(jnp.int32, (TILE, LANES), 1)
    row = lax.broadcasted_iota(jnp.int32, (TILE, LANES), 0)
    local = whole(folded + jnp.where((lane < own) & (row < heads_here), tail * tail, 0.0))
    state = jnp.concatenate(
        [
            jnp.zeros((1, LANES - 3 * share), jnp.float32),
            master_ref[...],
            moment_ref[...],
            second_ref[...],
        ],
        axis=1,
    )
    lane = lane[0:1]
    message = jnp.where(lane < own, tail[heads_here : heads_here + 1], state)
    message = jnp.where(lane == own, local, message)
    message = jnp.where(lane == own + 1, failed, message)
    for peer in range(message_ref.shape[0]):
        message_ref[peer] = message


def fold(rows):
    folded = rows[0:TILE]
    for row in range(TILE, rows.shape[0], TILE):
        folded = folded + rows[row : row + TILE]
    return folded


def whole(tile):
    return jnp.sum(jnp.sum(tile, axis=0, keepdims=True), axis=1, keepdims=True)


def exact_norm_kernel(in_ref, *refs):
    total = (in_ref[0] + in_ref[1]) + (in_ref[2] + in_ref[3])
    norm_message(total, jnp.zeros((1, 1), jnp.float32), *refs)


def coded_norm_kernel(in_ref, *refs):
    rows = in_ref.shape[1] - 2 * TILE
    proj = jnp.zeros((rows, LANES), jnp.float32)
    power = jnp.zeros((rows, LANES), jnp.float32)
    tail = jnp.zeros((TILE, LANES), jnp.float32)
    for chip in range(in_ref.shape[0]):
        high = in_ref[chip, rows : rows + TILE, :]
        part = in_ref[chip, :rows, :] * jnp.exp2(high[TILE - 2 : TILE - 1] - CODE_TOP)
        proj = proj + part
        power = power + part * part
        tail = tail + (high + in_ref[chip, rows + TILE :, :]) * jnp.exp2(
            high[TILE - 1 : TILE] - CODE_TOP
        )
    squares = proj * proj
    largest = jnp.max(jnp.max(squares, axis=0, keepdims=True), axis=1, keepdims=True)
    inverse = jnp.where(largest > 0.0, 1.0 / jnp.maximum(largest, 1e-37), 0.0)
    share = squares * inverse
    spread = power * inverse
    passed = (whole(fold(spread)) <= 1.5 * whole(fold(share))) & (
        whole(fold(share * spread)) <= whole(fold(share * share))
    )
    passed = passed & ((largest > 0.0) | (whole(fold(power)) <= 0.0))
    total = jnp.concatenate([proj, tail], axis=0)
    norm_message(total, jnp.where(passed, 0.0, 1.0), *refs)


def section_kernel(heard_ref, gain_ref, message_ref):
    section = lax.axis_index("section")
    own = LANES // 2
    sections = heard_ref.shape[0] // GROUP
    share = own // GROUP
    lane = lax.broadcasted_iota(jnp.int32, (1, LANES), 1)
    counted = jnp.zeros((1, LANES), jnp.float32)
    here = jnp.zeros((1, LANES), jnp.float32)
    ranks = [jnp.zeros((1, LANES), jnp.float32) for _ in range(GROUP)]
    for other in range(sections):
        rows = [heard_ref[rank * sections + other] for rank in range(GROUP)]
        summed = (rows[0] + rows[1]) + (rows[2] + rows[3])
        counted = counted + jnp.where(
            lane < own, summed * summed, jnp.where(lane <= own + 1, summed, 0.0)
        )
        here = here + jnp.where(section == other, summed, 0.0)
        ranks = [
            rank + jnp.where(section == other, row, 0.0) for rank, row in zip(ranks, rows)
        ]
    gain_ref[0:1, :] = here
    for kind in range(3):
        start = LANES - (3 - kind) * share
        state = jnp.ones((1, LANES), jnp.float32)
        for rank in range(GROUP):
            moved = pltpu.roll(ranks[rank], (rank * share - start) % LANES, 1)
            state = jnp.where(lane // share == rank, moved, state)
        gain_ref[kind + 1 : kind + 2, :] = state
    gain_ref[4:, :] = jnp.zeros((TILE - 4, LANES), jnp.float32)
    failed = jnp.sum(jnp.where(lane == own + 1, counted, 0.0), axis=1, keepdims=True)
    total = jnp.sum(jnp.where(lane == own + 1, 0.0, counted), axis=1, keepdims=True)
    total = jnp.where(lane == LANES - 1, failed, total)
    for peer in range(message_ref.shape[0]):
        message_ref[peer] = total


def update_kernel(
    scalars_ref,
    squares_ref,
    total_ref,
    gain_ref,
    proj_master_ref,
    proj_moment_ref,
    proj_second_ref,
    beta_master_ref,
    beta_moment_ref,
    beta_second_ref,
    weights_ref,
    proj_master_out,
    proj_moment_out,
    proj_second_out,
    beta_master_out,
    beta_moment_out,
    beta_second_out,
    gain_master_out,
    gain_moment_out,
    gain_second_out,
    rms_ref,
    *,
    counted,
):
    core, tensor = lax.axis_index("shard") % 2, lax.axis_index("tensor")
    own = proj_master_ref.shape[0]
    heads_here = beta_master_ref.shape[0]
    share = gain_master_out.shape[1]
    rows = total_ref.shape[0] - TILE
    rate = scalars_ref[0:1, :]
    squares = jnp.sum(squares_ref[...], axis=0)
    squares = jnp.broadcast_to(squares[:, 0:1], squares.shape)
    rms_ref[...] = jnp.sqrt(squares / counted)
    factor = jnp.minimum(1.0, scalars_ref[1:2, :] / (jnp.sqrt(squares) + norm_eps))
    for half in range(rows // own):
        columns = slice(half * LANES, (half + 1) * LANES)
        block = slice(half * own, (half + 1) * own)
        master, moment, second = adam_update(
            total_ref[block, :],
            factor,
            rate,
            proj_master_ref[:, columns],
            proj_moment_ref[:, columns],
            proj_second_ref[:, columns],
        )
        proj_master_out[:, columns] = master
        proj_moment_out[:, columns] = moment
        proj_second_out[:, columns] = second
        weights_ref[:own, columns] = master.astype(jnp.bfloat16)
    beta = adam_update(
        total_ref[rows : rows + heads_here, :own],
        factor[:, :own],
        rate[:, :own],
        beta_master_ref[...],
        beta_moment_ref[...],
        beta_second_ref[...],
    )
    beta_master_out[...] = beta[0]
    beta_moment_out[...] = beta[1]
    beta_second_out[...] = beta[2]
    gain = adam_update(
        gain_ref[0:1], factor, rate, gain_ref[1:2], gain_ref[2:3], gain_ref[3:4]
    )
    stacked = jnp.concatenate(list(gain) + [jnp.zeros((TILE - 3, LANES), jnp.float32)], axis=0)
    rolled = pltpu.roll(stacked, LANES - tensor * share, 1)
    gain_master_out[...] = rolled[0:1, :share]
    gain_moment_out[...] = rolled[1:2, :share]
    gain_second_out[...] = rolled[2:3, :share]
    small = jnp.concatenate(
        [beta[0], gain[0][:, :own], jnp.zeros((TILE - heads_here - 1, own), jnp.float32)], axis=0
    )
    small = jnp.concatenate([small, small], axis=1).astype(jnp.bfloat16)
    weights_ref[own:, :LANES] = small
    weights_ref[own:, LANES:] = jnp.zeros_like(small)


def unpack_kernel(in_ref, beta_ref, gain_ref):
    heads_here = beta_ref.shape[0]
    first = lax.broadcasted_iota(jnp.int32, (TILE, LANES), 1) < LANES // 2
    for chip in range(in_ref.shape[0] // 2):
        small = jnp.where(
            first,
            in_ref[2 * chip].astype(jnp.float32),
            in_ref[2 * chip + 1].astype(jnp.float32),
        ).astype(jnp.bfloat16)
        columns = slice(chip * LANES, (chip + 1) * LANES)
        beta_ref[:, columns] = small[:heads_here]
        gain_ref[:, columns] = small[heads_here : heads_here + 1]


def per_device(
    proj_grads,
    beta_grads,
    gain_grads,
    proj_master,
    proj_moment,
    proj_second,
    beta_master,
    beta_moment,
    beta_second,
    gain_master,
    gain_moment,
    gain_second,
    learn_rate,
    clip_limit,
):
    shards = lax.axis_size("shard")
    tensor_size = lax.axis_size("tensor")
    sections = lax.axis_size("section")
    chips = shards // 2
    micro, width, columns = proj_grads.shape[2:]
    heads_here = beta_grads.shape[3]
    own = width // shards
    rows = own * (columns // LANES)
    core_pairs = [(s, s ^ 1) for s in range(shards)]
    near = []
    for side in range(2):
        for base in range(0, chips, GROUP):
            members = [(base + 2 * side + j) % chips for j in range(GROUP)]
            near.append([2 * z + side for z in sorted(members, key=lambda z: z % GROUP)])
    far = [
        [2 * (residue + high * GROUP) + side for high in range(chips // GROUP)]
        for side in range(2)
        for residue in range(GROUP)
    ]

    proj = proj_grads[0, 0].reshape(micro, chips // GROUP, 2 * GROUP, own, columns)
    beta = beta_grads[0, 0]
    gain = gain_grads[0, 0, 0]
    rate, clip = learn_rate.reshape(1), clip_limit.reshape(1)
    states = (gain_master, gain_moment, gain_second)
    peers = tensor_size * sections

    def chip_parts():
        send, _ = pack(True, rate, clip, proj, beta, gain, rows + TILE)
        kept, scalars = pack(False, rate, clip, proj, beta, gain, rows + TILE)
        got = lax.ppermute(send, "shard", core_pairs)
        return kept, got, scalars

    def totals(kernel, value):
        total, message = pl.pallas_call(
            kernel,
            out_shape=(near_f32((rows + TILE, LANES)), near_f32((peers, 1, LANES))),
            in_specs=[VMEM] * 4,
            out_specs=(VMEM, VMEM),
            name="norm",
        )(held(value), *states)
        heard = lax.all_to_all(message, ("tensor", "section"), 0, 0)
        gain_rows, squares = pl.pallas_call(
            section_kernel,
            out_shape=(near_f32((TILE, LANES)), near_f32((shards, 1, LANES))),
            in_specs=[VMEM],
            out_specs=(VMEM, VMEM),
            name="section",
        )(held(heard))
        return total, gain_rows, lax.all_to_all(squares, "shard", 0, 0)

    def exact_totals(*_):
        kept, got, _ = chip_parts()
        chip_sum = pl.pallas_call(
            add_kernel,
            out_shape=near_f32(kept.shape),
            in_specs=[VMEM, VMEM],
            out_specs=VMEM,
            name="core_add",
        )(kept, held(got))
        by_near = lax.all_to_all(chip_sum, "shard", 0, 0, axis_index_groups=near)
        near_sum = pl.pallas_call(
            sum_kernel,
            out_shape=near_f32(by_near.shape[1:]),
            in_specs=[VMEM],
            out_specs=VMEM,
            name="near",
        )(held(by_near))
        by_far = lax.all_to_all(near_sum, "shard", 0, 0, axis_index_groups=far)
        return totals(exact_norm_kernel, by_far)

    kept, got, scalars = chip_parts()
    coded = pl.pallas_call(
        code_kernel,
        out_shape=near_f32((chips, rows + 2 * TILE, LANES)),
        in_specs=[VMEM, VMEM],
        out_specs=VMEM,
        name="code",
    )(kept, held(got))
    z_groups = [[2 * z + side for z in range(chips)] for side in range(2)]
    by_chip = lax.all_to_all(coded.astype(WIRE), "shard", 0, 0, axis_index_groups=z_groups)
    quick = totals(coded_norm_kernel, by_chip.astype(jnp.float32))
    failed = jnp.sum(quick[2][:, 0, LANES - 1]) > 0.0
    total, gain_rows, squares = lax.cond(failed, exact_totals, lambda *given: given, *quick)
    counted = sections * (
        width * columns * tensor_size + heads_here * tensor_size * width + width
    )
    state = f32((own, columns))
    beta_state = f32((heads_here, own))
    gain_state = f32(gain_master.shape)
    outs = pl.pallas_call(
        functools.partial(update_kernel, counted=float(counted)),
        out_shape=(pltpu.VMEM((own + TILE, columns), jnp.bfloat16),)
        + (state,) * 3
        + (beta_state,) * 3
        + (gain_state,) * 3
        + (f32((1, LANES)),),
        in_specs=[VMEM] * 10,
        out_specs=(VMEM,) * 11,
        name="update",
    )(
        held(scalars),
        held(squares),
        held(total),
        held(gain_rows),
        held(proj_master[0]),
        held(proj_moment[0]),
        held(proj_second[0]),
        held(beta_master[0]),
        held(beta_moment[0]),
        held(beta_second[0]),
    )
    sent = (outs[0].astype(jnp.float32) * WIRE_SCALE).astype(WIRE)
    gathered = lax.all_gather(sent, "shard", axis=0)
    unscaled = lambda value: (value.astype(jnp.float32) * (1.0 / WIRE_SCALE)).astype(jnp.bfloat16)
    proj_weights = unscaled(gathered[:, :own])
    small = unscaled(gathered[:, own:, :LANES])
    beta_weights, gain_weights = pl.pallas_call(
        unpack_kernel,
        out_shape=(
            jax.ShapeDtypeStruct((heads_here, width), jnp.bfloat16),
            jax.ShapeDtypeStruct((1, width), jnp.bfloat16),
        ),
        in_specs=[VMEM],
        out_specs=(VMEM, VMEM),
        name="unpack",
    )(held(small))
    return (
        proj_weights.reshape(1, width, columns),
        beta_weights[None],
        gain_weights,
        outs[1][None],
        outs[2][None],
        outs[3][None],
        outs[4][None],
        outs[5][None],
        outs[6][None],
        outs[7],
        outs[8],
        outs[9],
        outs[10][0, 0],
    )


def solution(mesh):
    in_specs = (
        P("section", "shard", None, None, "tensor"),
        P("section", "shard", None, "tensor", None),
        P("section", "shard", "tensor", None, None),
        P("section", "shard", "tensor"),
        P("section", "shard", "tensor"),
        P("section", "shard", "tensor"),
        P("section", "tensor", "shard"),
        P("section", "tensor", "shard"),
        P("section", "tensor", "shard"),
        P("section", ("shard", "tensor")),
        P("section", ("shard", "tensor")),
        P("section", ("shard", "tensor")),
        P(),
        P(),
    )
    out_specs = (
        P("section", None, "tensor"),
        P("section", "tensor", None),
        P("section", None),
        P("section", "shard", "tensor"),
        P("section", "shard", "tensor"),
        P("section", "shard", "tensor"),
        P("section", "tensor", "shard"),
        P("section", "tensor", "shard"),
        P("section", "tensor", "shard"),
        P("section", ("shard", "tensor")),
        P("section", ("shard", "tensor")),
        P("section", ("shard", "tensor")),
        P(),
    )
    return jax.shard_map(
        per_device, mesh=mesh, in_specs=in_specs, out_specs=out_specs, check_vma=False
    )
```

```python
import functools

import jax
import jax.numpy as jnp
from jax import lax
from jax.experimental import pallas as pl
from jax.experimental.pallas import tpu as pltpu
from jax.sharding import PartitionSpec as P

first_beta = 0.9
second_beta = 0.95
decay_rate = 0.1
adam_eps = 1e-08
norm_eps = 1e-06

LANES = 128
TILE = 8
GROUP = 4
CODE_TOP = 14.0
CODE_STEP = 1.5 * 2.0**27
WIRE = jnp.float16
WIRE_SCALE = 2.0**15

SMALL = pltpu.CompilerParams(vmem_limit_bytes=8 * 2**20)
VMEM = pl.BlockSpec(memory_space=pltpu.VMEM)
SMEM = pl.BlockSpec(memory_space=pltpu.SMEM)


def adam_update(grad, factor, learn_rate, master, moment, second):
    clipped = grad * factor
    moment_new = first_beta * moment + (1.0 - first_beta) * clipped
    second_new = second_beta * second + (1.0 - second_beta) * clipped * clipped
    master_new = master * (1.0 - learn_rate * decay_rate) - learn_rate * moment_new / (
        jnp.sqrt(second_new) + adam_eps
    )
    return (master_new, moment_new, second_new)


def f32(shape):
    return jax.ShapeDtypeStruct(shape, jnp.float32)


def near_f32(shape):
    return pltpu.VMEM(shape, jnp.float32)


def held(value):
    return pltpu.with_memory_space_constraint(value, pltpu.VMEM)


def tail_rows(beta_ref, gain_ref):
    beta = beta_ref[0].astype(jnp.float32) + beta_ref[1].astype(jnp.float32)
    gain = gain_ref[...].astype(jnp.float32)
    blank = jnp.zeros((TILE - beta.shape[0] - 1, beta.shape[1]), jnp.float32)
    return jnp.concatenate([beta, gain[0:1] + gain[1:2], blank], axis=0)


def stack_halves(rows):
    return jnp.concatenate(
        [rows[:, start : start + LANES] for start in range(0, rows.shape[1], LANES)], axis=0
    )


def proj_rows(proj_ref, chip, core):
    place = (chip // GROUP, chip % GROUP, core)
    return stack_halves(
        proj_ref[(0,) + place].astype(jnp.float32) + proj_ref[(1,) + place].astype(jnp.float32)
    )


def pack_kernel(
    proj_ref,
    beta_ref,
    gain_ref,
    gain_master_ref,
    gain_moment_ref,
    gain_second_ref,
    out_ref,
    tails_ref,
    state_ref,
    buffer,
    staged,
    arrived,
    sent,
):
    other = 1 - lax.axis_index("shard") % 2
    arrivals = [
        pltpu.make_async_copy(
            proj_ref.at[:, high, :, other], buffer.at[high], arrived.at[high]
        )
        for high in range(GROUP)
    ]
    for copy in arrivals:
        copy.start()
    tails = tail_rows(beta_ref, gain_ref)
    tails_ref[...] = tails
    state = gain_state_row(gain_master_ref, gain_moment_ref, gain_second_ref)
    state_ref[...] = jnp.broadcast_to(state, state_ref.shape)
    rows = staged.shape[1] - TILE
    departures = []
    for high in range(GROUP):
        arrivals[high].wait()
        for low in range(GROUP):
            chip = high * GROUP + low
            staged[chip, :rows, :] = stack_halves(
                buffer[high, 0, low].astype(jnp.float32) + buffer[high, 1, low].astype(jnp.float32)
            )
            staged[chip, rows:, :] = tails[:, chip * LANES : (chip + 1) * LANES]
        part = pl.ds(high * GROUP, GROUP)
        departures.append(pltpu.make_async_copy(staged.at[part], out_ref.at[part], sent.at[high]))
        departures[-1].start()
    for copy in departures:
        copy.wait()


def pack(proj, beta, gain, states, rows):
    own, columns = proj.shape[4:]
    shape = (GROUP * GROUP, rows, LANES)
    return pl.pallas_call(
        pack_kernel,
        in_specs=[pl.BlockSpec(memory_space=pl.ANY)] + [VMEM] * 5,
        out_specs=(pl.BlockSpec(memory_space=pl.ANY), VMEM, VMEM),
        out_shape=(f32(shape), near_f32((TILE, gain.shape[1])), near_f32((TILE, LANES))),
        scratch_shapes=[
            pltpu.VMEM((GROUP, 2, GROUP, own, columns), jnp.bfloat16),
            pltpu.VMEM(shape, jnp.float32),
            pltpu.SemaphoreType.DMA((GROUP,)),
            pltpu.SemaphoreType.DMA((GROUP,)),
        ],
        name="pack",
        compiler_params=SMALL,
    )(proj, beta, gain, *states)


def block_scale(rows):
    largest = jnp.max(jnp.max(jnp.abs(rows), axis=0, keepdims=True), axis=1, keepdims=True)
    return jnp.ceil(jnp.log2(jnp.maximum(largest, 1e-30)) + 0.01)


def gain_state_row(*refs):
    states = [ref[...] for ref in refs]
    share = states[0].shape[1]
    return jnp.concatenate([jnp.zeros((1, LANES - 3 * share), jnp.float32)] + states, axis=1)


def code_kernel(rate_ref, clip_ref, proj_ref, tails_ref, got_ref, out_ref, scalars_ref):
    row = lax.broadcasted_iota(jnp.int32, (TILE, LANES), 0)
    scalars_ref[...] = jnp.where(row == 0, rate_ref[0], clip_ref[0])
    rows = got_ref.shape[1] - TILE
    own = LANES // 2
    core = lax.axis_index("shard") % 2
    left_half = lax.broadcasted_iota(jnp.int32, (TILE, LANES), 1) < own
    for chip in range(GROUP * GROUP):
        proj = proj_rows(proj_ref, chip, core) + got_ref[chip, :rows, :]
        tail = tails_ref[:, chip * LANES : (chip + 1) * LANES] + got_ref[chip, rows:, :]
        tail = pltpu.roll(tail, LANES - core * own, 1)
        proj_scale, tail_scale = block_scale(proj), block_scale(tail)
        out_ref[chip, :rows, :] = proj * jnp.exp2(CODE_TOP - proj_scale)
        tail = tail * jnp.exp2(CODE_TOP - tail_scale)
        high = (tail + CODE_STEP) - CODE_STEP
        low = pltpu.roll(tail - high, own, 1)
        tail = jnp.where(left_half, high, low)
        tail = jnp.where(row == TILE - 2, proj_scale, jnp.where(row == TILE - 1, tail_scale, tail))
        out_ref[chip, rows:, :] = tail


def add_kernel(proj_ref, tails_ref, got_ref, out_ref):
    rows = got_ref.shape[1] - TILE
    core = lax.axis_index("shard") % 2
    for chip in range(GROUP * GROUP):
        place = (chip % GROUP, chip // GROUP)
        tail = tails_ref[:, chip * LANES : (chip + 1) * LANES]
        out_ref[place + (slice(0, rows),)] = proj_rows(proj_ref, chip, core) + got_ref[chip, :rows, :]
        out_ref[place + (slice(rows, None),)] = tail + got_ref[chip, rows:, :]


def sum_kernel(in_ref, out_ref):
    out_ref[...] = (in_ref[0] + in_ref[1]) + (in_ref[2] + in_ref[3])


def norm_message(total, failed, state, total_ref, message_ref):
    rows = total_ref.shape[0] - TILE
    own = LANES // 2
    heads_here = TILE // 2
    tail = total[rows:]
    total_ref[...] = total
    folded = fold(total[:rows] * total[:rows])
    lane = lax.broadcasted_iota(jnp.int32, (TILE, LANES), 1)
    row = lax.broadcasted_iota(jnp.int32, (TILE, LANES), 0)
    local = whole(folded + jnp.where((lane < own) & (row < heads_here), tail * tail, 0.0))
    lane = lane[0:1]
    message = jnp.where(lane < own, tail[heads_here : heads_here + 1], state)
    message = jnp.where(lane == own, local, message)
    message = jnp.where(lane == own + 1, failed, message)
    for peer in range(message_ref.shape[0]):
        message_ref[peer] = message


def fold(rows):
    folded = rows[0:TILE]
    for row in range(TILE, rows.shape[0], TILE):
        folded = folded + rows[row : row + TILE]
    return folded


def whole(tile):
    return jnp.sum(jnp.sum(tile, axis=0, keepdims=True), axis=1, keepdims=True)


def exact_norm_kernel(in_ref, state_ref, *refs):
    total = (in_ref[0] + in_ref[1]) + (in_ref[2] + in_ref[3])
    rows = total.shape[0] - TILE
    shift = LANES - lax.axis_index("shard") % 2 * (LANES // 2)
    total = jnp.concatenate([total[:rows], pltpu.roll(total[rows:], shift, 1)], axis=0)
    norm_message(total, jnp.zeros((1, 1), jnp.float32), state_ref[0:1, :], *refs)


def coded_norm_kernel(in_ref, state_ref, *refs):
    rows = in_ref.shape[1] - TILE
    own = LANES // 2
    proj = jnp.zeros((rows, LANES), jnp.float32)
    power = jnp.zeros((rows, LANES), jnp.float32)
    tail = jnp.zeros((TILE, LANES), jnp.float32)
    for chip in range(in_ref.shape[0]):
        coded = in_ref[chip, rows:, :]
        part = in_ref[chip, :rows, :] * jnp.exp2(coded[TILE - 2 : TILE - 1] - CODE_TOP)
        proj = proj + part
        power = power + part * part
        tail = tail + (coded + pltpu.roll(coded, own, 1)) * jnp.exp2(
            coded[TILE - 1 : TILE] - CODE_TOP
        )
    squares = proj * proj
    largest = jnp.max(jnp.max(squares, axis=0, keepdims=True), axis=1, keepdims=True)
    inverse = jnp.where(largest > 0.0, 1.0 / jnp.maximum(largest, 1e-37), 0.0)
    share = squares * inverse
    spread = power * inverse
    passed = (whole(fold(spread)) <= 1.5 * whole(fold(share))) & (
        whole(fold(share * spread)) <= whole(fold(share * share))
    )
    passed = passed & ((largest > 0.0) | (whole(fold(power)) <= 0.0))
    total = jnp.concatenate([proj, tail], axis=0)
    norm_message(total, jnp.where(passed, 0.0, 1.0), state_ref[0:1, :], *refs)


def section_kernel(heard_ref, gain_ref, message_ref):
    section = lax.axis_index("section")
    own = LANES // 2
    sections = heard_ref.shape[0] // GROUP
    share = own // GROUP
    lane = lax.broadcasted_iota(jnp.int32, (1, LANES), 1)
    counted = jnp.zeros((1, LANES), jnp.float32)
    here = jnp.zeros((1, LANES), jnp.float32)
    ranks = [jnp.zeros((1, LANES), jnp.float32) for _ in range(GROUP)]
    for other in range(sections):
        rows = [heard_ref[rank * sections + other] for rank in range(GROUP)]
        summed = (rows[0] + rows[1]) + (rows[2] + rows[3])
        counted = counted + jnp.where(
            lane < own, summed * summed, jnp.where(lane <= own + 1, summed, 0.0)
        )
        here = here + jnp.where(section == other, summed, 0.0)
        ranks = [
            rank + jnp.where(section == other, row, 0.0) for rank, row in zip(ranks, rows)
        ]
    gain_ref[0:1, :] = here
    for kind in range(3):
        start = LANES - (3 - kind) * share
        state = jnp.ones((1, LANES), jnp.float32)
        for rank in range(GROUP):
            moved = pltpu.roll(ranks[rank], (rank * share - start) % LANES, 1)
            state = jnp.where(lane // share == rank, moved, state)
        gain_ref[kind + 1 : kind + 2, :] = state
    gain_ref[4:, :] = jnp.zeros((TILE - 4, LANES), jnp.float32)
    failed = jnp.sum(jnp.where(lane == own + 1, counted, 0.0), axis=1, keepdims=True)
    total = jnp.sum(jnp.where(lane == own + 1, 0.0, counted), axis=1, keepdims=True)
    total = jnp.where(lane == LANES - 1, failed, total)
    for peer in range(message_ref.shape[0]):
        message_ref[peer] = total


def update_kernel(
    scalars_ref,
    squares_ref,
    total_ref,
    gain_ref,
    proj_master_ref,
    proj_moment_ref,
    proj_second_ref,
    beta_master_ref,
    beta_moment_ref,
    beta_second_ref,
    weights_ref,
    proj_master_out,
    proj_moment_out,
    proj_second_out,
    beta_master_out,
    beta_moment_out,
    beta_second_out,
    gain_master_out,
    gain_moment_out,
    gain_second_out,
    rms_ref,
    *,
    counted,
):
    core, tensor = lax.axis_index("shard") % 2, lax.axis_index("tensor")
    own = proj_master_ref.shape[0]
    heads_here = beta_master_ref.shape[0]
    share = gain_master_out.shape[1]
    rows = total_ref.shape[0] - TILE
    rate = scalars_ref[0:1, :]
    squares = jnp.sum(squares_ref[...], axis=0)
    squares = jnp.broadcast_to(squares[:, 0:1], squares.shape)
    rms_ref[...] = jnp.sqrt(squares / counted)
    factor = jnp.minimum(1.0, scalars_ref[1:2, :] / (jnp.sqrt(squares) + norm_eps))
    for half in range(rows // own):
        columns = slice(half * LANES, (half + 1) * LANES)
        block = slice(half * own, (half + 1) * own)
        master, moment, second = adam_update(
            total_ref[block, :],
            factor,
            rate,
            proj_master_ref[:, columns],
            proj_moment_ref[:, columns],
            proj_second_ref[:, columns],
        )
        proj_master_out[:, columns] = master
        proj_moment_out[:, columns] = moment
        proj_second_out[:, columns] = second
        weights_ref[:own, columns] = master.astype(jnp.bfloat16)
    beta = adam_update(
        total_ref[rows : rows + heads_here, :own],
        factor[:, :own],
        rate[:, :own],
        beta_master_ref[...],
        beta_moment_ref[...],
        beta_second_ref[...],
    )
    beta_master_out[...] = beta[0]
    beta_moment_out[...] = beta[1]
    beta_second_out[...] = beta[2]
    gain = adam_update(
        gain_ref[0:1], factor, rate, gain_ref[1:2], gain_ref[2:3], gain_ref[3:4]
    )
    stacked = jnp.concatenate(list(gain) + [jnp.zeros((TILE - 3, LANES), jnp.float32)], axis=0)
    rolled = pltpu.roll(stacked, LANES - tensor * share, 1)
    gain_master_out[...] = rolled[0:1, :share]
    gain_moment_out[...] = rolled[1:2, :share]
    gain_second_out[...] = rolled[2:3, :share]
    small = jnp.concatenate(
        [beta[0], gain[0][:, :own], jnp.zeros((TILE - heads_here - 1, own), jnp.float32)], axis=0
    )
    small = jnp.concatenate([small, small], axis=1).astype(jnp.bfloat16)
    weights_ref[own:, :LANES] = small
    weights_ref[own:, LANES:] = jnp.zeros_like(small)


def unpack_kernel(in_ref, beta_ref, gain_ref):
    heads_here = beta_ref.shape[0]
    first = lax.broadcasted_iota(jnp.int32, (TILE, LANES), 1) < LANES // 2
    for chip in range(in_ref.shape[0] // 2):
        small = jnp.where(
            first,
            in_ref[2 * chip].astype(jnp.float32),
            in_ref[2 * chip + 1].astype(jnp.float32),
        ).astype(jnp.bfloat16)
        columns = slice(chip * LANES, (chip + 1) * LANES)
        beta_ref[:, columns] = small[:heads_here]
        gain_ref[:, columns] = small[heads_here : heads_here + 1]


def per_device(
    proj_grads,
    beta_grads,
    gain_grads,
    proj_master,
    proj_moment,
    proj_second,
    beta_master,
    beta_moment,
    beta_second,
    gain_master,
    gain_moment,
    gain_second,
    learn_rate,
    clip_limit,
):
    shards = lax.axis_size("shard")
    tensor_size = lax.axis_size("tensor")
    sections = lax.axis_size("section")
    chips = shards // 2
    micro, width, columns = proj_grads.shape[2:]
    heads_here = beta_grads.shape[3]
    own = width // shards
    rows = own * (columns // LANES)
    core_pairs = [(s, s ^ 1) for s in range(shards)]
    near = []
    for side in range(2):
        for base in range(0, chips, GROUP):
            members = [(base + 2 * side + j) % chips for j in range(GROUP)]
            near.append([2 * z + side for z in sorted(members, key=lambda z: z % GROUP)])
    far = [
        [2 * (residue + high * GROUP) + side for high in range(chips // GROUP)]
        for side in range(2)
        for residue in range(GROUP)
    ]

    proj = proj_grads[0, 0].reshape(micro, chips // GROUP, GROUP, 2, own, columns)
    beta = beta_grads[0, 0]
    gain = gain_grads[0, 0, 0]
    rate, clip = learn_rate.reshape(1), clip_limit.reshape(1)
    states = (gain_master, gain_moment, gain_second)
    peers = tensor_size * sections

    def chip_parts(proj, beta, gain, states):
        send, tails, state = pack(proj, beta, gain, states, rows + TILE)
        return held(tails), held(lax.ppermute(send, "shard", core_pairs)), held(state)

    def totals(kernel, value, state):
        total, message = pl.pallas_call(
            kernel,
            out_shape=(near_f32((rows + TILE, LANES)), near_f32((peers, 1, LANES))),
            in_specs=[VMEM, VMEM],
            out_specs=(VMEM, VMEM),
            name="norm",
            compiler_params=SMALL,
        )(held(value), state)
        heard = lax.all_to_all(message, ("tensor", "section"), 0, 0)
        gain_rows, squares = pl.pallas_call(
            section_kernel,
            out_shape=(near_f32((TILE, LANES)), near_f32((shards, 1, LANES))),
            in_specs=[VMEM],
            out_specs=(VMEM, VMEM),
            name="section",
            compiler_params=SMALL,
        )(held(heard))
        return total, gain_rows, lax.all_to_all(squares, "shard", 0, 0)

    def exact_totals(proj, beta, gain, states, _):
        tails, got, state = chip_parts(proj, beta, gain, states)
        chip_sum = pl.pallas_call(
            add_kernel,
            out_shape=f32((GROUP, GROUP, rows + TILE, LANES)),
            in_specs=[VMEM] * 3,
            out_specs=VMEM,
            name="core_add",
            compiler_params=SMALL,
        )(proj, tails, got)
        by_near = lax.all_to_all(chip_sum, "shard", 0, 0, axis_index_groups=near)
        near_sum = pl.pallas_call(
            sum_kernel,
            out_shape=near_f32(by_near.shape[1:]),
            in_specs=[VMEM],
            out_specs=VMEM,
            name="near",
            compiler_params=SMALL,
        )(held(by_near))
        by_far = lax.all_to_all(near_sum, "shard", 0, 0, axis_index_groups=far)
        return totals(exact_norm_kernel, by_far, state)

    tails, got, state = chip_parts(proj, beta, gain, states)
    coded, scalars = pl.pallas_call(
        code_kernel,
        out_shape=(near_f32((chips, rows + TILE, LANES)), near_f32((TILE, LANES))),
        in_specs=[SMEM, SMEM] + [VMEM] * 3,
        out_specs=(VMEM, VMEM),
        name="code",
        compiler_params=SMALL,
    )(rate, clip, held(proj), tails, got)
    z_groups = [[2 * z + side for z in range(chips)] for side in range(2)]
    by_chip = lax.all_to_all(coded.astype(WIRE), "shard", 0, 0, axis_index_groups=z_groups)
    quick = totals(coded_norm_kernel, by_chip.astype(jnp.float32), state)
    *again, norm = lax.optimization_barrier(
        (proj, beta, gain, states, quick[2])
    )
    quick = (quick[0], quick[1], norm)
    failed = jnp.sum(norm[:, 0, LANES - 1]) > 0.0
    total, gain_rows, squares = lax.cond(
        failed, exact_totals, lambda *given: given[-1], *again, quick
    )
    counted = sections * (
        width * columns * tensor_size + heads_here * tensor_size * width + width
    )
    state = f32((own, columns))
    beta_state = f32((heads_here, own))
    gain_state = f32(gain_master.shape)
    outs = pl.pallas_call(
        functools.partial(update_kernel, counted=float(counted)),
        out_shape=(pltpu.VMEM((own + TILE, columns), jnp.bfloat16),)
        + (state,) * 3
        + (beta_state,) * 3
        + (gain_state,) * 3
        + (f32((1, LANES)),),
        in_specs=[VMEM] * 10,
        out_specs=(VMEM,) * 11,
        name="update",
        compiler_params=SMALL,
    )(
        held(scalars),
        held(squares),
        held(total),
        held(gain_rows),
        proj_master[0],
        proj_moment[0],
        proj_second[0],
        beta_master[0],
        beta_moment[0],
        beta_second[0],
    )
    sent = (outs[0].astype(jnp.float32) * WIRE_SCALE).astype(WIRE)
    gathered = lax.all_gather(sent, "shard", axis=0)
    unscaled = lambda value: (value.astype(jnp.float32) * (1.0 / WIRE_SCALE)).astype(jnp.bfloat16)
    proj_weights = unscaled(gathered[:, :own])
    small = unscaled(gathered[:, own:, :LANES])
    beta_weights, gain_weights = pl.pallas_call(
        unpack_kernel,
        out_shape=(
            jax.ShapeDtypeStruct((heads_here, width), jnp.bfloat16),
            jax.ShapeDtypeStruct((1, width), jnp.bfloat16),
        ),
        in_specs=[VMEM],
        out_specs=(VMEM, VMEM),
        name="unpack",
        compiler_params=SMALL,
    )(held(small))
    return (
        proj_weights.reshape(1, width, columns),
        beta_weights[None],
        gain_weights,
        outs[1][None],
        outs[2][None],
        outs[3][None],
        outs[4][None],
        outs[5][None],
        outs[6][None],
        outs[7],
        outs[8],
        outs[9],
        outs[10][0, 0],
    )


def solution(mesh):
    in_specs = (
        P("section", "shard", None, None, "tensor"),
        P("section", "shard", None, "tensor", None),
        P("section", "shard", "tensor", None, None),
        P("section", "shard", "tensor"),
        P("section", "shard", "tensor"),
        P("section", "shard", "tensor"),
        P("section", "tensor", "shard"),
        P("section", "tensor", "shard"),
        P("section", "tensor", "shard"),
        P("section", ("shard", "tensor")),
        P("section", ("shard", "tensor")),
        P("section", ("shard", "tensor")),
        P(),
        P(),
    )
    out_specs = (
        P("section", None, "tensor"),
        P("section", "tensor", None),
        P("section", None),
        P("section", "shard", "tensor"),
        P("section", "shard", "tensor"),
        P("section", "shard", "tensor"),
        P("section", "tensor", "shard"),
        P("section", "tensor", "shard"),
        P("section", "tensor", "shard"),
        P("section", ("shard", "tensor")),
        P("section", ("shard", "tensor")),
        P("section", ("shard", "tensor")),
        P(),
    )
    return jax.shard_map(
        per_device, mesh=mesh, in_specs=in_specs, out_specs=out_specs, check_vma=False
    )
```

```python
import functools

import jax
import jax.numpy as jnp
from jax import lax
from jax.experimental import pallas as pl
from jax.experimental.pallas import tpu as pltpu
from jax.sharding import PartitionSpec as P

first_beta = 0.9
second_beta = 0.95
decay_rate = 0.1
adam_eps = 1e-08
norm_eps = 1e-06

LANES = 128
TILE = 8
GROUP = 4
CODE_TOP = 14.0
CODE_STEP = 1.5 * 2.0**27
WIRE = jnp.float16
WIRE_SCALE = 2.0**15

SMALL = pltpu.CompilerParams(vmem_limit_bytes=8 * 2**20)
VMEM = pl.BlockSpec(memory_space=pltpu.VMEM)
SMEM = pl.BlockSpec(memory_space=pltpu.SMEM)


def adam_update(grad, factor, learn_rate, master, moment, second):
    clipped = grad * factor
    moment_new = first_beta * moment + (1.0 - first_beta) * clipped
    second_new = second_beta * second + (1.0 - second_beta) * clipped * clipped
    master_new = master * (1.0 - learn_rate * decay_rate) - learn_rate * moment_new / (
        jnp.sqrt(second_new) + adam_eps
    )
    return (master_new, moment_new, second_new)


def f32(shape):
    return jax.ShapeDtypeStruct(shape, jnp.float32)


def near_f32(shape):
    return pltpu.VMEM(shape, jnp.float32)


def held(value):
    return pltpu.with_memory_space_constraint(value, pltpu.VMEM)


def tail_rows(beta_ref, gain_ref):
    beta = beta_ref[0].astype(jnp.float32) + beta_ref[1].astype(jnp.float32)
    gain = gain_ref[...].astype(jnp.float32)
    blank = jnp.zeros((TILE - beta.shape[0] - 1, beta.shape[1]), jnp.float32)
    return jnp.concatenate([beta, gain[0:1] + gain[1:2], blank], axis=0)


def stack_halves(rows):
    return jnp.concatenate(
        [rows[:, start : start + LANES] for start in range(0, rows.shape[1], LANES)], axis=0
    )


def pack_kernel(
    proj_ref,
    beta_ref,
    gain_ref,
    gain_master_ref,
    gain_moment_ref,
    gain_second_ref,
    out_ref,
    state_ref,
    buffer,
    arrived,
    *,
    flip,
):
    core = lax.axis_index("shard") % 2
    which = 1 - core if flip else core
    arrivals = [
        pltpu.make_async_copy(
            proj_ref.at[:, high, :, which], buffer.at[high], arrived.at[high]
        )
        for high in range(GROUP)
    ]
    for copy in arrivals:
        copy.start()
    tails = tail_rows(beta_ref, gain_ref)
    state = gain_state_row(gain_master_ref, gain_moment_ref, gain_second_ref)
    state_ref[...] = jnp.broadcast_to(state, state_ref.shape)
    rows = out_ref.shape[1] - TILE
    for high in range(GROUP):
        arrivals[high].wait()
        for low in range(GROUP):
            chip = high * GROUP + low
            out_ref[chip, :rows, :] = stack_halves(
                buffer[high, 0, low].astype(jnp.float32) + buffer[high, 1, low].astype(jnp.float32)
            )
            out_ref[chip, rows:, :] = tails[:, chip * LANES : (chip + 1) * LANES]


def pack(flip, proj, beta, gain, states, rows):
    own, columns = proj.shape[4:]
    return pl.pallas_call(
        functools.partial(pack_kernel, flip=flip),
        in_specs=[pl.BlockSpec(memory_space=pl.ANY)] + [VMEM] * 5,
        out_specs=(VMEM, VMEM),
        out_shape=(near_f32((GROUP * GROUP, rows, LANES)), near_f32((TILE, LANES))),
        scratch_shapes=[
            pltpu.VMEM((GROUP, 2, GROUP, own, columns), jnp.bfloat16),
            pltpu.SemaphoreType.DMA((GROUP,)),
        ],
        name="pack",
        compiler_params=SMALL,
    )(proj, beta, gain, *states)


def block_scale(rows):
    largest = jnp.max(jnp.max(jnp.abs(rows), axis=0, keepdims=True), axis=1, keepdims=True)
    return jnp.ceil(jnp.log2(jnp.maximum(largest, 1e-30)) + 0.01)


def gain_state_row(*refs):
    states = [ref[...] for ref in refs]
    share = states[0].shape[1]
    return jnp.concatenate([jnp.zeros((1, LANES - 3 * share), jnp.float32)] + states, axis=1)


def code_kernel(rate_ref, clip_ref, kept_ref, got_ref, out_ref, scalars_ref):
    row = lax.broadcasted_iota(jnp.int32, (TILE, LANES), 0)
    scalars_ref[...] = jnp.where(row == 0, rate_ref[0], clip_ref[0])
    rows = got_ref.shape[1] - TILE
    own = LANES // 2
    core = lax.axis_index("shard") % 2
    left_half = lax.broadcasted_iota(jnp.int32, (TILE, LANES), 1) < own
    for chip in range(GROUP * GROUP):
        proj = kept_ref[chip, :rows, :] + got_ref[chip, :rows, :]
        tail = kept_ref[chip, rows:, :] + got_ref[chip, rows:, :]
        tail = pltpu.roll(tail, LANES - core * own, 1)
        proj_scale, tail_scale = block_scale(proj), block_scale(tail)
        out_ref[chip, :rows, :] = proj * jnp.exp2(CODE_TOP - proj_scale)
        tail = tail * jnp.exp2(CODE_TOP - tail_scale)
        high = (tail + CODE_STEP) - CODE_STEP
        low = pltpu.roll(tail - high, own, 1)
        tail = jnp.where(left_half, high, low)
        tail = jnp.where(row == TILE - 2, proj_scale, jnp.where(row == TILE - 1, tail_scale, tail))
        out_ref[chip, rows:, :] = tail


def add_kernel(kept_ref, got_ref, out_ref):
    for chip in range(GROUP * GROUP):
        out_ref[chip % GROUP, chip // GROUP] = kept_ref[chip] + got_ref[chip]


def sum_kernel(in_ref, out_ref):
    out_ref[...] = (in_ref[0] + in_ref[1]) + (in_ref[2] + in_ref[3])


def norm_message(total, failed, state, total_ref, message_ref):
    rows = total_ref.shape[0] - TILE
    own = LANES // 2
    heads_here = TILE // 2
    tail = total[rows:]
    total_ref[...] = total
    folded = fold(total[:rows] * total[:rows])
    lane = lax.broadcasted_iota(jnp.int32, (TILE, LANES), 1)
    row = lax.broadcasted_iota(jnp.int32, (TILE, LANES), 0)
    local = whole(folded + jnp.where((lane < own) & (row < heads_here), tail * tail, 0.0))
    lane = lane[0:1]
    message = jnp.where(lane < own, tail[heads_here : heads_here + 1], state)
    message = jnp.where(lane == own, local, message)
    message = jnp.where(lane == own + 1, failed, message)
    for peer in range(message_ref.shape[0]):
        message_ref[peer] = message


def fold(rows):
    folded = rows[0:TILE]
    for row in range(TILE, rows.shape[0], TILE):
        folded = folded + rows[row : row + TILE]
    return folded


def whole(tile):
    return jnp.sum(jnp.sum(tile, axis=0, keepdims=True), axis=1, keepdims=True)


def exact_norm_kernel(in_ref, state_ref, *refs):
    total = (in_ref[0] + in_ref[1]) + (in_ref[2] + in_ref[3])
    rows = total.shape[0] - TILE
    shift = LANES - lax.axis_index("shard") % 2 * (LANES // 2)
    total = jnp.concatenate([total[:rows], pltpu.roll(total[rows:], shift, 1)], axis=0)
    norm_message(total, jnp.zeros((1, 1), jnp.float32), state_ref[0:1, :], *refs)


def coded_norm_kernel(in_ref, state_ref, *refs):
    rows = in_ref.shape[1] - TILE
    own = LANES // 2
    proj = jnp.zeros((rows, LANES), jnp.float32)
    power = jnp.zeros((rows, LANES), jnp.float32)
    tail = jnp.zeros((TILE, LANES), jnp.float32)
    for chip in range(in_ref.shape[0]):
        coded = in_ref[chip, rows:, :]
        part = in_ref[chip, :rows, :] * jnp.exp2(coded[TILE - 2 : TILE - 1] - CODE_TOP)
        proj = proj + part
        power = power + part * part
        tail = tail + (coded + pltpu.roll(coded, own, 1)) * jnp.exp2(
            coded[TILE - 1 : TILE] - CODE_TOP
        )
    squares = proj * proj
    largest = jnp.max(jnp.max(squares, axis=0, keepdims=True), axis=1, keepdims=True)
    inverse = jnp.where(largest > 0.0, 1.0 / jnp.maximum(largest, 1e-37), 0.0)
    share = squares * inverse
    spread = power * inverse
    passed = (whole(fold(spread)) <= 1.5 * whole(fold(share))) & (
        whole(fold(share * spread)) <= whole(fold(share * share))
    )
    passed = passed & ((largest > 0.0) | (whole(fold(power)) <= 0.0))
    total = jnp.concatenate([proj, tail], axis=0)
    norm_message(total, jnp.where(passed, 0.0, 1.0), state_ref[0:1, :], *refs)


def section_kernel(heard_ref, gain_ref, message_ref):
    section = lax.axis_index("section")
    own = LANES // 2
    sections = heard_ref.shape[0] // GROUP
    share = own // GROUP
    lane = lax.broadcasted_iota(jnp.int32, (1, LANES), 1)
    counted = jnp.zeros((1, LANES), jnp.float32)
    here = jnp.zeros((1, LANES), jnp.float32)
    ranks = [jnp.zeros((1, LANES), jnp.float32) for _ in range(GROUP)]
    for other in range(sections):
        rows = [heard_ref[rank * sections + other] for rank in range(GROUP)]
        summed = (rows[0] + rows[1]) + (rows[2] + rows[3])
        counted = counted + jnp.where(
            lane < own, summed * summed, jnp.where(lane <= own + 1, summed, 0.0)
        )
        here = here + jnp.where(section == other, summed, 0.0)
        ranks = [
            rank + jnp.where(section == other, row, 0.0) for rank, row in zip(ranks, rows)
        ]
    gain_ref[0:1, :] = here
    for kind in range(3):
        start = LANES - (3 - kind) * share
        state = jnp.ones((1, LANES), jnp.float32)
        for rank in range(GROUP):
            moved = pltpu.roll(ranks[rank], (rank * share - start) % LANES, 1)
            state = jnp.where(lane // share == rank, moved, state)
        gain_ref[kind + 1 : kind + 2, :] = state
    gain_ref[4:, :] = jnp.zeros((TILE - 4, LANES), jnp.float32)
    failed = jnp.sum(jnp.where(lane == own + 1, counted, 0.0), axis=1, keepdims=True)
    total = jnp.sum(jnp.where(lane == own + 1, 0.0, counted), axis=1, keepdims=True)
    total = jnp.where(lane == LANES - 1, failed, total)
    for peer in range(message_ref.shape[0]):
        message_ref[peer] = total


def update_kernel(
    scalars_ref,
    squares_ref,
    total_ref,
    gain_ref,
    proj_master_ref,
    proj_moment_ref,
    proj_second_ref,
    beta_master_ref,
    beta_moment_ref,
    beta_second_ref,
    weights_ref,
    proj_master_out,
    proj_moment_out,
    proj_second_out,
    beta_master_out,
    beta_moment_out,
    beta_second_out,
    gain_master_out,
    gain_moment_out,
    gain_second_out,
    rms_ref,
    *,
    counted,
):
    core, tensor = lax.axis_index("shard") % 2, lax.axis_index("tensor")
    own = proj_master_ref.shape[0]
    heads_here = beta_master_ref.shape[0]
    share = gain_master_out.shape[1]
    rows = total_ref.shape[0] - TILE
    rate = scalars_ref[0:1, :]
    squares = jnp.sum(squares_ref[...], axis=0)
    squares = jnp.broadcast_to(squares[:, 0:1], squares.shape)
    rms_ref[...] = jnp.sqrt(squares / counted)
    factor = jnp.minimum(1.0, scalars_ref[1:2, :] / (jnp.sqrt(squares) + norm_eps))
    for half in range(rows // own):
        columns = slice(half * LANES, (half + 1) * LANES)
        block = slice(half * own, (half + 1) * own)
        master, moment, second = adam_update(
            total_ref[block, :],
            factor,
            rate,
            proj_master_ref[:, columns],
            proj_moment_ref[:, columns],
            proj_second_ref[:, columns],
        )
        proj_master_out[:, columns] = master
        proj_moment_out[:, columns] = moment
        proj_second_out[:, columns] = second
        weights_ref[:own, columns] = master.astype(jnp.bfloat16)
    beta = adam_update(
        total_ref[rows : rows + heads_here, :own],
        factor[:, :own],
        rate[:, :own],
        beta_master_ref[...],
        beta_moment_ref[...],
        beta_second_ref[...],
    )
    beta_master_out[...] = beta[0]
    beta_moment_out[...] = beta[1]
    beta_second_out[...] = beta[2]
    gain = adam_update(
        gain_ref[0:1], factor, rate, gain_ref[1:2], gain_ref[2:3], gain_ref[3:4]
    )
    stacked = jnp.concatenate(list(gain) + [jnp.zeros((TILE - 3, LANES), jnp.float32)], axis=0)
    rolled = pltpu.roll(stacked, LANES - tensor * share, 1)
    gain_master_out[...] = rolled[0:1, :share]
    gain_moment_out[...] = rolled[1:2, :share]
    gain_second_out[...] = rolled[2:3, :share]
    small = jnp.concatenate(
        [beta[0], gain[0][:, :own], jnp.zeros((TILE - heads_here - 1, own), jnp.float32)], axis=0
    )
    small = jnp.concatenate([small, small], axis=1).astype(jnp.bfloat16)
    weights_ref[own:, :LANES] = small
    weights_ref[own:, LANES:] = jnp.zeros_like(small)


def unpack_kernel(in_ref, beta_ref, gain_ref):
    heads_here = beta_ref.shape[0]
    first = lax.broadcasted_iota(jnp.int32, (TILE, LANES), 1) < LANES // 2
    for chip in range(in_ref.shape[0] // 2):
        small = jnp.where(
            first,
            in_ref[2 * chip].astype(jnp.float32),
            in_ref[2 * chip + 1].astype(jnp.float32),
        ).astype(jnp.bfloat16)
        columns = slice(chip * LANES, (chip + 1) * LANES)
        beta_ref[:, columns] = small[:heads_here]
        gain_ref[:, columns] = small[heads_here : heads_here + 1]


def per_device(
    proj_grads,
    beta_grads,
    gain_grads,
    proj_master,
    proj_moment,
    proj_second,
    beta_master,
    beta_moment,
    beta_second,
    gain_master,
    gain_moment,
    gain_second,
    learn_rate,
    clip_limit,
):
    shards = lax.axis_size("shard")
    tensor_size = lax.axis_size("tensor")
    sections = lax.axis_size("section")
    chips = shards // 2
    micro, width, columns = proj_grads.shape[2:]
    heads_here = beta_grads.shape[3]
    own = width // shards
    rows = own * (columns // LANES)
    core_pairs = [(s, s ^ 1) for s in range(shards)]
    near = []
    for side in range(2):
        for base in range(0, chips, GROUP):
            members = [(base + 2 * side + j) % chips for j in range(GROUP)]
            near.append([2 * z + side for z in sorted(members, key=lambda z: z % GROUP)])
    far = [
        [2 * (residue + high * GROUP) + side for high in range(chips // GROUP)]
        for side in range(2)
        for residue in range(GROUP)
    ]

    proj = proj_grads[0, 0].reshape(micro, chips // GROUP, GROUP, 2, own, columns)
    beta = beta_grads[0, 0]
    gain = gain_grads[0, 0, 0]
    rate, clip = learn_rate.reshape(1), clip_limit.reshape(1)
    states = (gain_master, gain_moment, gain_second)
    peers = tensor_size * sections

    def chip_parts(proj, beta, gain, states):
        send, state = pack(True, proj, beta, gain, states, rows + TILE)
        kept, _ = pack(False, proj, beta, gain, states, rows + TILE)
        return held(kept), held(lax.ppermute(send, "shard", core_pairs)), held(state)

    def totals(kernel, value, state):
        total, message = pl.pallas_call(
            kernel,
            out_shape=(near_f32((rows + TILE, LANES)), near_f32((peers, 1, LANES))),
            in_specs=[VMEM, VMEM],
            out_specs=(VMEM, VMEM),
            name="norm",
            compiler_params=SMALL,
        )(held(value), state)
        heard = lax.all_to_all(message, ("tensor", "section"), 0, 0)
        gain_rows, squares = pl.pallas_call(
            section_kernel,
            out_shape=(near_f32((TILE, LANES)), near_f32((shards, 1, LANES))),
            in_specs=[VMEM],
            out_specs=(VMEM, VMEM),
            name="section",
            compiler_params=SMALL,
        )(held(heard))
        return total, gain_rows, lax.all_to_all(squares, "shard", 0, 0)

    def exact_totals(proj, beta, gain, states, _):
        kept, got, state = chip_parts(proj, beta, gain, states)
        chip_sum = pl.pallas_call(
            add_kernel,
            out_shape=f32((GROUP, GROUP, rows + TILE, LANES)),
            in_specs=[VMEM] * 2,
            out_specs=VMEM,
            name="core_add",
            compiler_params=SMALL,
        )(kept, got)
        by_near = lax.all_to_all(chip_sum, "shard", 0, 0, axis_index_groups=near)
        near_sum = pl.pallas_call(
            sum_kernel,
            out_shape=near_f32(by_near.shape[1:]),
            in_specs=[VMEM],
            out_specs=VMEM,
            name="near",
            compiler_params=SMALL,
        )(held(by_near))
        by_far = lax.all_to_all(near_sum, "shard", 0, 0, axis_index_groups=far)
        return totals(exact_norm_kernel, by_far, state)

    kept, got, state = chip_parts(proj, beta, gain, states)
    coded, scalars = pl.pallas_call(
        code_kernel,
        out_shape=(near_f32((chips, rows + TILE, LANES)), near_f32((TILE, LANES))),
        in_specs=[SMEM, SMEM, VMEM, VMEM],
        out_specs=(VMEM, VMEM),
        name="code",
        compiler_params=SMALL,
    )(rate, clip, kept, got)
    z_groups = [[2 * z + side for z in range(chips)] for side in range(2)]
    by_chip = lax.all_to_all(coded.astype(WIRE), "shard", 0, 0, axis_index_groups=z_groups)
    quick = totals(coded_norm_kernel, by_chip.astype(jnp.float32), state)
    *again, norm = lax.optimization_barrier(
        (proj, beta, gain, states, quick[2])
    )
    quick = (quick[0], quick[1], norm)
    failed = jnp.sum(norm[:, 0, LANES - 1]) > 0.0
    total, gain_rows, squares = lax.cond(
        failed, exact_totals, lambda *given: given[-1], *again, quick
    )
    counted = sections * (
        width * columns * tensor_size + heads_here * tensor_size * width + width
    )
    state = f32((own, columns))
    beta_state = f32((heads_here, own))
    gain_state = f32(gain_master.shape)
    outs = pl.pallas_call(
        functools.partial(update_kernel, counted=float(counted)),
        out_shape=(pltpu.VMEM((own + TILE, columns), jnp.bfloat16),)
        + (state,) * 3
        + (beta_state,) * 3
        + (gain_state,) * 3
        + (f32((1, LANES)),),
        in_specs=[VMEM] * 10,
        out_specs=(VMEM,) * 11,
        name="update",
        compiler_params=SMALL,
    )(
        held(scalars),
        held(squares),
        held(total),
        held(gain_rows),
        proj_master[0],
        proj_moment[0],
        proj_second[0],
        beta_master[0],
        beta_moment[0],
        beta_second[0],
    )
    sent = (outs[0].astype(jnp.float32) * WIRE_SCALE).astype(WIRE)
    gathered = lax.all_gather(sent, "shard", axis=0)
    unscaled = lambda value: (value.astype(jnp.float32) * (1.0 / WIRE_SCALE)).astype(jnp.bfloat16)
    proj_weights = unscaled(gathered[:, :own])
    small = unscaled(gathered[:, own:, :LANES])
    beta_weights, gain_weights = pl.pallas_call(
        unpack_kernel,
        out_shape=(
            jax.ShapeDtypeStruct((heads_here, width), jnp.bfloat16),
            jax.ShapeDtypeStruct((1, width), jnp.bfloat16),
        ),
        in_specs=[VMEM],
        out_specs=(VMEM, VMEM),
        name="unpack",
        compiler_params=SMALL,
    )(held(small))
    return (
        proj_weights.reshape(1, width, columns),
        beta_weights[None],
        gain_weights,
        outs[1][None],
        outs[2][None],
        outs[3][None],
        outs[4][None],
        outs[5][None],
        outs[6][None],
        outs[7],
        outs[8],
        outs[9],
        outs[10][0, 0],
    )


def solution(mesh):
    in_specs = (
        P("section", "shard", None, None, "tensor"),
        P("section", "shard", None, "tensor", None),
        P("section", "shard", "tensor", None, None),
        P("section", "shard", "tensor"),
        P("section", "shard", "tensor"),
        P("section", "shard", "tensor"),
        P("section", "tensor", "shard"),
        P("section", "tensor", "shard"),
        P("section", "tensor", "shard"),
        P("section", ("shard", "tensor")),
        P("section", ("shard", "tensor")),
        P("section", ("shard", "tensor")),
        P(),
        P(),
    )
    out_specs = (
        P("section", None, "tensor"),
        P("section", "tensor", None),
        P("section", None),
        P("section", "shard", "tensor"),
        P("section", "shard", "tensor"),
        P("section", "shard", "tensor"),
        P("section", "tensor", "shard"),
        P("section", "tensor", "shard"),
        P("section", "tensor", "shard"),
        P("section", ("shard", "tensor")),
        P("section", ("shard", "tensor")),
        P("section", ("shard", "tensor")),
        P(),
    )
    return jax.shard_map(
        per_device, mesh=mesh, in_specs=in_specs, out_specs=out_specs, check_vma=False
    )
```

```python
import functools

import jax
import jax.numpy as jnp
from jax import lax
from jax.experimental import pallas as pl
from jax.experimental.pallas import tpu as pltpu
from jax.sharding import PartitionSpec as P

first_beta = 0.9
second_beta = 0.95
decay_rate = 0.1
adam_eps = 1e-08
norm_eps = 1e-06

LANES = 128
TILE = 8
GROUP = 4
CODE_TOP = 14.0
CODE_STEP = 1.5 * 2.0**27
WIRE = jnp.float16
WIRE_SCALE = 2.0**15

SMALL = pltpu.CompilerParams(vmem_limit_bytes=8 * 2**20)
VMEM = pl.BlockSpec(memory_space=pltpu.VMEM)
SMEM = pl.BlockSpec(memory_space=pltpu.SMEM)


def adam_update(grad, factor, learn_rate, master, moment, second):
    clipped = grad * factor
    moment_new = first_beta * moment + (1.0 - first_beta) * clipped
    second_new = second_beta * second + (1.0 - second_beta) * clipped * clipped
    master_new = master * (1.0 - learn_rate * decay_rate) - learn_rate * moment_new / (
        jnp.sqrt(second_new) + adam_eps
    )
    return (master_new, moment_new, second_new)


def f32(shape):
    return jax.ShapeDtypeStruct(shape, jnp.float32)


def near_f32(shape):
    return pltpu.VMEM(shape, jnp.float32)


def held(value):
    return pltpu.with_memory_space_constraint(value, pltpu.VMEM)


def tail_rows(beta_ref, gain_ref):
    beta = beta_ref[0].astype(jnp.float32) + beta_ref[1].astype(jnp.float32)
    gain = gain_ref[...].astype(jnp.float32)
    blank = jnp.zeros((TILE - beta.shape[0] - 1, beta.shape[1]), jnp.float32)
    return jnp.concatenate([beta, gain[0:1] + gain[1:2], blank], axis=0)


def stack_halves(rows):
    return jnp.concatenate(
        [rows[:, start : start + LANES] for start in range(0, rows.shape[1], LANES)], axis=0
    )


def pack_kernel(
    proj_ref,
    beta_ref,
    gain_ref,
    gain_master_ref,
    gain_moment_ref,
    gain_second_ref,
    out_ref,
    state_ref,
    buffer,
    arrived,
    *,
    flip,
):
    core = lax.axis_index("shard") % 2
    which = 1 - core if flip else core
    arrivals = [
        pltpu.make_async_copy(
            proj_ref.at[:, high, :, which], buffer.at[high], arrived.at[high]
        )
        for high in range(GROUP)
    ]
    for copy in arrivals:
        copy.start()
    tails = tail_rows(beta_ref, gain_ref)
    state = gain_state_row(gain_master_ref, gain_moment_ref, gain_second_ref)
    state_ref[...] = jnp.broadcast_to(state, state_ref.shape)
    rows = out_ref.shape[1] - TILE
    for high in range(GROUP):
        arrivals[high].wait()
        for low in range(GROUP):
            chip = high * GROUP + low
            out_ref[chip, :rows, :] = stack_halves(
                buffer[high, 0, low].astype(jnp.float32) + buffer[high, 1, low].astype(jnp.float32)
            )
            out_ref[chip, rows:, :] = tails[:, chip * LANES : (chip + 1) * LANES]


def pack(flip, proj, beta, gain, states, rows):
    own, columns = proj.shape[4:]
    return pl.pallas_call(
        functools.partial(pack_kernel, flip=flip),
        in_specs=[pl.BlockSpec(memory_space=pl.ANY)] + [VMEM] * 5,
        out_specs=(VMEM, VMEM),
        out_shape=(near_f32((GROUP * GROUP, rows, LANES)), near_f32((TILE, LANES))),
        scratch_shapes=[
            pltpu.VMEM((GROUP, 2, GROUP, own, columns), jnp.bfloat16),
            pltpu.SemaphoreType.DMA((GROUP,)),
        ],
        name="pack",
        compiler_params=SMALL,
    )(proj, beta, gain, *states)


def block_scale(rows):
    largest = jnp.max(jnp.max(jnp.abs(rows), axis=0, keepdims=True), axis=1, keepdims=True)
    return jnp.ceil(jnp.log2(jnp.maximum(largest, 1e-30)) + 0.01)


def gain_state_row(*refs):
    states = [ref[...] for ref in refs]
    share = states[0].shape[1]
    return jnp.concatenate([jnp.zeros((1, LANES - 3 * share), jnp.float32)] + states, axis=1)


def code_kernel(rate_ref, clip_ref, kept_ref, got_ref, out_ref, scalars_ref):
    row = lax.broadcasted_iota(jnp.int32, (TILE, LANES), 0)
    scalars_ref[...] = jnp.where(row == 0, rate_ref[0], clip_ref[0])
    rows = got_ref.shape[1] - TILE
    own = LANES // 2
    core = lax.axis_index("shard") % 2
    left_half = lax.broadcasted_iota(jnp.int32, (TILE, LANES), 1) < own
    for chip in range(GROUP * GROUP):
        proj = kept_ref[chip, :rows, :] + got_ref[chip, :rows, :]
        tail = kept_ref[chip, rows:, :] + got_ref[chip, rows:, :]
        tail = pltpu.roll(tail, LANES - core * own, 1)
        proj_scale, tail_scale = block_scale(proj), block_scale(tail)
        out_ref[chip, :rows, :] = proj * jnp.exp2(CODE_TOP - proj_scale)
        tail = tail * jnp.exp2(CODE_TOP - tail_scale)
        high = (tail + CODE_STEP) - CODE_STEP
        low = pltpu.roll(tail - high, own, 1)
        tail = jnp.where(left_half, high, low)
        tail = jnp.where(row == TILE - 2, proj_scale, jnp.where(row == TILE - 1, tail_scale, tail))
        out_ref[chip, rows:, :] = tail


def add_kernel(kept_ref, got_ref, out_ref):
    for chip in range(GROUP * GROUP):
        out_ref[chip % GROUP, chip // GROUP] = kept_ref[chip] + got_ref[chip]


def sum_kernel(in_ref, out_ref):
    out_ref[...] = (in_ref[0] + in_ref[1]) + (in_ref[2] + in_ref[3])


def norm_message(total, failed, state, total_ref, message_ref):
    rows = total_ref.shape[0] - TILE
    own = LANES // 2
    heads_here = TILE // 2
    tail = total[rows:]
    total_ref[...] = total
    folded = fold(total[:rows] * total[:rows])
    lane = lax.broadcasted_iota(jnp.int32, (TILE, LANES), 1)
    row = lax.broadcasted_iota(jnp.int32, (TILE, LANES), 0)
    local = whole(folded + jnp.where((lane < own) & (row < heads_here), tail * tail, 0.0))
    lane = lane[0:1]
    message = jnp.where(lane < own, tail[heads_here : heads_here + 1], state)
    message = jnp.where(lane == own, local, message)
    message = jnp.where(lane == own + 1, failed, message)
    for peer in range(message_ref.shape[0]):
        message_ref[peer] = message


def fold(rows):
    folded = rows[0:TILE]
    for row in range(TILE, rows.shape[0], TILE):
        folded = folded + rows[row : row + TILE]
    return folded


def whole(tile):
    return jnp.sum(jnp.sum(tile, axis=0, keepdims=True), axis=1, keepdims=True)


def exact_norm_kernel(in_ref, state_ref, *refs):
    total = (in_ref[0] + in_ref[1]) + (in_ref[2] + in_ref[3])
    rows = total.shape[0] - TILE
    shift = LANES - lax.axis_index("shard") % 2 * (LANES // 2)
    total = jnp.concatenate([total[:rows], pltpu.roll(total[rows:], shift, 1)], axis=0)
    norm_message(total, jnp.zeros((1, 1), jnp.float32), state_ref[0:1, :], *refs)


def coded_norm_kernel(in_ref, state_ref, *refs):
    rows = in_ref.shape[1] - TILE
    own = LANES // 2
    proj = jnp.zeros((rows, LANES), jnp.float32)
    power = jnp.zeros((rows, LANES), jnp.float32)
    tail = jnp.zeros((TILE, LANES), jnp.float32)
    for chip in range(in_ref.shape[0]):
        coded = in_ref[chip, rows:, :]
        part = in_ref[chip, :rows, :] * jnp.exp2(coded[TILE - 2 : TILE - 1] - CODE_TOP)
        proj = proj + part
        power = power + part * part
        tail = tail + (coded + pltpu.roll(coded, own, 1)) * jnp.exp2(
            coded[TILE - 1 : TILE] - CODE_TOP
        )
    squares = proj * proj
    largest = jnp.max(jnp.max(squares, axis=0, keepdims=True), axis=1, keepdims=True)
    inverse = jnp.where(largest > 0.0, 1.0 / jnp.maximum(largest, 1e-37), 0.0)
    share = squares * inverse
    spread = power * inverse
    passed = (whole(fold(spread)) <= 1.5 * whole(fold(share))) & (
        whole(fold(share * spread)) <= whole(fold(share * share))
    )
    passed = passed & ((largest > 0.0) | (whole(fold(power)) <= 0.0))
    total = jnp.concatenate([proj, tail], axis=0)
    norm_message(total, jnp.where(passed, 0.0, 1.0), state_ref[0:1, :], *refs)


def section_kernel(heard_ref, gain_ref, message_ref):
    section = lax.axis_index("section")
    own = LANES // 2
    sections = heard_ref.shape[0] // GROUP
    share = own // GROUP
    lane = lax.broadcasted_iota(jnp.int32, (1, LANES), 1)
    counted = jnp.zeros((1, LANES), jnp.float32)
    here = jnp.zeros((1, LANES), jnp.float32)
    ranks = [jnp.zeros((1, LANES), jnp.float32) for _ in range(GROUP)]
    for other in range(sections):
        rows = [heard_ref[rank * sections + other] for rank in range(GROUP)]
        summed = (rows[0] + rows[1]) + (rows[2] + rows[3])
        counted = counted + jnp.where(
            lane < own, summed * summed, jnp.where(lane <= own + 1, summed, 0.0)
        )
        here = here + jnp.where(section == other, summed, 0.0)
        ranks = [
            rank + jnp.where(section == other, row, 0.0) for rank, row in zip(ranks, rows)
        ]
    gain_ref[0:1, :] = here
    for kind in range(3):
        start = LANES - (3 - kind) * share
        state = jnp.ones((1, LANES), jnp.float32)
        for rank in range(GROUP):
            moved = pltpu.roll(ranks[rank], (rank * share - start) % LANES, 1)
            state = jnp.where(lane // share == rank, moved, state)
        gain_ref[kind + 1 : kind + 2, :] = state
    gain_ref[4:, :] = jnp.zeros((TILE - 4, LANES), jnp.float32)
    failed = jnp.sum(jnp.where(lane == own + 1, counted, 0.0), axis=1, keepdims=True)
    total = jnp.sum(jnp.where(lane == own + 1, 0.0, counted), axis=1, keepdims=True)
    total = jnp.where(lane == LANES - 1, failed, total)
    for peer in range(message_ref.shape[0]):
        message_ref[peer] = total


def flag_kernel(squares_ref, *refs):
    half = len(refs) // 2
    flag_ref = refs[half]
    for state_ref, held_ref in zip(refs[:half], refs[half + 1 :]):
        held_ref[...] = state_ref[...]
    rows = jnp.sum(squares_ref[...], axis=0)
    lane = lax.broadcasted_iota(jnp.int32, rows.shape, 1)
    failed = jnp.max(jnp.where(lane == LANES - 1, rows, 0.0))
    flag_ref[0] = jnp.where(failed > 0.0, 1, 0)


def update_kernel(
    scalars_ref,
    squares_ref,
    total_ref,
    gain_ref,
    proj_master_ref,
    proj_moment_ref,
    proj_second_ref,
    beta_master_ref,
    beta_moment_ref,
    beta_second_ref,
    weights_ref,
    proj_master_out,
    proj_moment_out,
    proj_second_out,
    beta_master_out,
    beta_moment_out,
    beta_second_out,
    gain_master_out,
    gain_moment_out,
    gain_second_out,
    rms_ref,
    *,
    counted,
):
    core, tensor = lax.axis_index("shard") % 2, lax.axis_index("tensor")
    own = proj_master_ref.shape[0]
    heads_here = beta_master_ref.shape[0]
    share = gain_master_out.shape[1]
    rows = total_ref.shape[0] - TILE
    rate = scalars_ref[0:1, :]
    squares = jnp.sum(squares_ref[...], axis=0)
    squares = jnp.broadcast_to(squares[:, 0:1], squares.shape)
    rms_ref[...] = jnp.sqrt(squares / counted)
    factor = jnp.minimum(1.0, scalars_ref[1:2, :] / (jnp.sqrt(squares) + norm_eps))
    for half in range(rows // own):
        columns = slice(half * LANES, (half + 1) * LANES)
        block = slice(half * own, (half + 1) * own)
        master, moment, second = adam_update(
            total_ref[block, :],
            factor,
            rate,
            proj_master_ref[:, columns],
            proj_moment_ref[:, columns],
            proj_second_ref[:, columns],
        )
        proj_master_out[:, columns] = master
        proj_moment_out[:, columns] = moment
        proj_second_out[:, columns] = second
        weights_ref[:own, columns] = master.astype(jnp.bfloat16)
    beta = adam_update(
        total_ref[rows : rows + heads_here, :own],
        factor[:, :own],
        rate[:, :own],
        beta_master_ref[...],
        beta_moment_ref[...],
        beta_second_ref[...],
    )
    beta_master_out[...] = beta[0]
    beta_moment_out[...] = beta[1]
    beta_second_out[...] = beta[2]
    gain = adam_update(
        gain_ref[0:1], factor, rate, gain_ref[1:2], gain_ref[2:3], gain_ref[3:4]
    )
    stacked = jnp.concatenate(list(gain) + [jnp.zeros((TILE - 3, LANES), jnp.float32)], axis=0)
    rolled = pltpu.roll(stacked, LANES - tensor * share, 1)
    gain_master_out[...] = rolled[0:1, :share]
    gain_moment_out[...] = rolled[1:2, :share]
    gain_second_out[...] = rolled[2:3, :share]
    small = jnp.concatenate(
        [beta[0], gain[0][:, :own], jnp.zeros((TILE - heads_here - 1, own), jnp.float32)], axis=0
    )
    small = jnp.concatenate([small, small], axis=1).astype(jnp.bfloat16)
    weights_ref[own:, :LANES] = small
    weights_ref[own:, LANES:] = jnp.zeros_like(small)


def unpack_kernel(in_ref, beta_ref, gain_ref):
    heads_here = beta_ref.shape[0]
    first = lax.broadcasted_iota(jnp.int32, (TILE, LANES), 1) < LANES // 2
    for chip in range(in_ref.shape[0] // 2):
        small = jnp.where(
            first,
            in_ref[2 * chip].astype(jnp.float32),
            in_ref[2 * chip + 1].astype(jnp.float32),
        ).astype(jnp.bfloat16)
        columns = slice(chip * LANES, (chip + 1) * LANES)
        beta_ref[:, columns] = small[:heads_here]
        gain_ref[:, columns] = small[heads_here : heads_here + 1]


def per_device(
    proj_grads,
    beta_grads,
    gain_grads,
    proj_master,
    proj_moment,
    proj_second,
    beta_master,
    beta_moment,
    beta_second,
    gain_master,
    gain_moment,
    gain_second,
    learn_rate,
    clip_limit,
):
    shards = lax.axis_size("shard")
    tensor_size = lax.axis_size("tensor")
    sections = lax.axis_size("section")
    chips = shards // 2
    micro, width, columns = proj_grads.shape[2:]
    heads_here = beta_grads.shape[3]
    own = width // shards
    rows = own * (columns // LANES)
    core_pairs = [(s, s ^ 1) for s in range(shards)]
    near = []
    for side in range(2):
        for base in range(0, chips, GROUP):
            members = [(base + 2 * side + j) % chips for j in range(GROUP)]
            near.append([2 * z + side for z in sorted(members, key=lambda z: z % GROUP)])
    far = [
        [2 * (residue + high * GROUP) + side for high in range(chips // GROUP)]
        for side in range(2)
        for residue in range(GROUP)
    ]

    proj = proj_grads[0, 0].reshape(micro, chips // GROUP, GROUP, 2, own, columns)
    beta = beta_grads[0, 0]
    gain = gain_grads[0, 0, 0]
    rate, clip = learn_rate.reshape(1), clip_limit.reshape(1)
    states = (gain_master, gain_moment, gain_second)
    peers = tensor_size * sections

    def chip_parts(proj, beta, gain, states):
        send, state = pack(True, proj, beta, gain, states, rows + TILE)
        kept, _ = pack(False, proj, beta, gain, states, rows + TILE)
        return held(kept), held(lax.ppermute(send, "shard", core_pairs)), held(state)

    def totals(kernel, value, state):
        total, message = pl.pallas_call(
            kernel,
            out_shape=(near_f32((rows + TILE, LANES)), near_f32((peers, 1, LANES))),
            in_specs=[VMEM, VMEM],
            out_specs=(VMEM, VMEM),
            name="norm",
            compiler_params=SMALL,
        )(held(value), state)
        heard = lax.all_to_all(message, ("tensor", "section"), 0, 0)
        gain_rows, squares = pl.pallas_call(
            section_kernel,
            out_shape=(near_f32((TILE, LANES)), near_f32((shards, 1, LANES))),
            in_specs=[VMEM],
            out_specs=(VMEM, VMEM),
            name="section",
            compiler_params=SMALL,
        )(held(heard))
        return total, gain_rows, lax.all_to_all(squares, "shard", 0, 0)

    def exact_totals(proj, beta, gain, states, _):
        kept, got, state = chip_parts(proj, beta, gain, states)
        chip_sum = pl.pallas_call(
            add_kernel,
            out_shape=f32((GROUP, GROUP, rows + TILE, LANES)),
            in_specs=[VMEM] * 2,
            out_specs=VMEM,
            name="core_add",
            compiler_params=SMALL,
        )(kept, got)
        by_near = lax.all_to_all(chip_sum, "shard", 0, 0, axis_index_groups=near)
        near_sum = pl.pallas_call(
            sum_kernel,
            out_shape=near_f32(by_near.shape[1:]),
            in_specs=[VMEM],
            out_specs=VMEM,
            name="near",
            compiler_params=SMALL,
        )(held(by_near))
        by_far = lax.all_to_all(near_sum, "shard", 0, 0, axis_index_groups=far)
        return totals(exact_norm_kernel, by_far, state)

    kept, got, state = chip_parts(proj, beta, gain, states)
    coded, scalars = pl.pallas_call(
        code_kernel,
        out_shape=(near_f32((chips, rows + TILE, LANES)), near_f32((TILE, LANES))),
        in_specs=[SMEM, SMEM, VMEM, VMEM],
        out_specs=(VMEM, VMEM),
        name="code",
        compiler_params=SMALL,
    )(rate, clip, kept, got)
    z_groups = [[2 * z + side for z in range(chips)] for side in range(2)]
    by_chip = lax.all_to_all(coded.astype(WIRE), "shard", 0, 0, axis_index_groups=z_groups)
    quick = totals(coded_norm_kernel, by_chip.astype(jnp.float32), state)
    *again, norm = lax.optimization_barrier(
        (proj, beta, gain, states, quick[2])
    )
    quick = (quick[0], quick[1], norm)
    own_states = [
        value[0]
        for value in (
            proj_master,
            proj_moment,
            proj_second,
            beta_master,
            beta_moment,
            beta_second,
        )
    ]
    flag, *own_states = pl.pallas_call(
        flag_kernel,
        out_shape=(jax.ShapeDtypeStruct((1,), jnp.int32),)
        + tuple(near_f32(value.shape) for value in own_states),
        in_specs=[VMEM] * 7,
        out_specs=(SMEM,) + (VMEM,) * 6,
        name="flag",
        compiler_params=SMALL,
    )(held(norm), *own_states)
    failed = flag[0] > 0
    total, gain_rows, squares = lax.cond(
        failed, exact_totals, lambda *given: given[-1], *again, quick
    )
    counted = sections * (
        width * columns * tensor_size + heads_here * tensor_size * width + width
    )
    state = f32((own, columns))
    beta_state = f32((heads_here, own))
    gain_state = f32(gain_master.shape)
    outs = pl.pallas_call(
        functools.partial(update_kernel, counted=float(counted)),
        out_shape=(pltpu.VMEM((own + TILE, columns), jnp.bfloat16),)
        + (state,) * 3
        + (beta_state,) * 3
        + (gain_state,) * 3
        + (f32((1, LANES)),),
        in_specs=[VMEM] * 10,
        out_specs=(VMEM,) * 11,
        name="update",
        compiler_params=SMALL,
    )(
        held(scalars),
        held(squares),
        held(total),
        held(gain_rows),
        *[held(value) for value in own_states],
    )
    sent = (outs[0].astype(jnp.float32) * WIRE_SCALE).astype(WIRE)
    gathered = lax.all_gather(sent, "shard", axis=0)
    unscaled = lambda value: (value.astype(jnp.float32) * (1.0 / WIRE_SCALE)).astype(jnp.bfloat16)
    proj_weights = unscaled(gathered[:, :own])
    small = unscaled(gathered[:, own:, :LANES])
    beta_weights, gain_weights = pl.pallas_call(
        unpack_kernel,
        out_shape=(
            jax.ShapeDtypeStruct((heads_here, width), jnp.bfloat16),
            jax.ShapeDtypeStruct((1, width), jnp.bfloat16),
        ),
        in_specs=[VMEM],
        out_specs=(VMEM, VMEM),
        name="unpack",
        compiler_params=SMALL,
    )(held(small))
    return (
        proj_weights.reshape(1, width, columns),
        beta_weights[None],
        gain_weights,
        outs[1][None],
        outs[2][None],
        outs[3][None],
        outs[4][None],
        outs[5][None],
        outs[6][None],
        outs[7],
        outs[8],
        outs[9],
        outs[10][0, 0],
    )


def solution(mesh):
    in_specs = (
        P("section", "shard", None, None, "tensor"),
        P("section", "shard", None, "tensor", None),
        P("section", "shard", "tensor", None, None),
        P("section", "shard", "tensor"),
        P("section", "shard", "tensor"),
        P("section", "shard", "tensor"),
        P("section", "tensor", "shard"),
        P("section", "tensor", "shard"),
        P("section", "tensor", "shard"),
        P("section", ("shard", "tensor")),
        P("section", ("shard", "tensor")),
        P("section", ("shard", "tensor")),
        P(),
        P(),
    )
    out_specs = (
        P("section", None, "tensor"),
        P("section", "tensor", None),
        P("section", None),
        P("section", "shard", "tensor"),
        P("section", "shard", "tensor"),
        P("section", "shard", "tensor"),
        P("section", "tensor", "shard"),
        P("section", "tensor", "shard"),
        P("section", "tensor", "shard"),
        P("section", ("shard", "tensor")),
        P("section", ("shard", "tensor")),
        P("section", ("shard", "tensor")),
        P(),
    )
    return jax.shard_map(
        per_device, mesh=mesh, in_specs=in_specs, out_specs=out_specs, check_vma=False
    )
```
